32 devices in a mesh: wide: 8 (over z, x), narrow: 4 (over y, core).
Axes of the slice: x: 2, y: 2, z: 4, core: 2. Of those that a mesh axis runs over, the one named last changes fastest.
Arguments:
- density: bfloat16 [4096, 4096], P('wide', 'narrow'), may hold values from -0.0059814453 to 0.0059814453
- block_slot: int32 [32], replicated, may hold values from 0 to 31, as said below
- region_blocks: int32 [512], P(('wide', 'narrow')), may hold values from 0 to 31, as said below
- basis_lists: int32 [384, 8], P(('wide', 'narrow')), may hold values from 0 to 15, as said below
- point_counts: int32 [384], P(('wide', 'narrow')), may hold values from 1 to 256
- orbitals: bfloat16 [384, 1024, 256], P(('wide', 'narrow')), may hold values from -6 to 6
- weights: float32 [384, 256], P(('wide', 'narrow')), may hold values from 0.01 to 0.1
- harmonics: bfloat16 [384, 64, 256], P(('wide', 'narrow')), may hold values from -32 to 32
Outputs:
- hamiltonian: float32 [4096, 4096], P('wide', 'narrow')
The draws below stay inside these ranges and needn't reach their ends.
Inputs may be any that keep to these rules, and one draw needn't show every extreme that they name: `block_slot`: a permutation of the 32 layout slots. `region_blocks`: the 16 blocks of one region are distinct; among the 256 block pairs of one region, no owner of the layout holds more than 8, and some owner holds exactly 8. `basis_lists`: the 8 positions of one list are distinct.
All inputs are finite; a program needn't handle non-finite values.
Results may differ from the reference program's by a relative error of at most 0.0023.
Values may be sent and summed in bfloat16 or wider, within the bound.
A program may use at most 128 MiB of HBM per device.

```python
import math
import jax
import jax.numpy as jnp
from jax import lax

BLK = 128
PTS = 256
K = 8
S = 16
NL = 64
QB = 4
BATCH_DEV = 12
NB = 32
BATCHES = 384
TOTAL_PTS = 98304
N_WIDE = 8
N_NARROW = 4


def slot_table(key):
    return jax.random.permutation(jax.random.fold_in(key, 11), NB).astype(jnp.int32)


def draw_block_slot(key, part):
    return slot_table(key)


def draw_region_blocks(key, part):
    devices_all = N_WIDE * N_NARROW
    table = slot_table(key)
    inverse = jnp.argsort(table).astype(jnp.int32)
    starts = jax.random.randint(jax.random.fold_in(key, 12), (devices_all,), 0, N_WIDE)
    offsets = jnp.arange(S)
    residue = (starts[:, None] + offsets[None, :]) % N_WIDE
    q_pick = jax.random.randint(jax.random.fold_in(key, 13), (devices_all, N_WIDE), 0, QB)
    q_base = q_pick[:, offsets % N_WIDE]
    q_value = (q_base + (offsets // N_WIDE)[None, :]) % QB
    slots = q_value * N_WIDE + residue
    return inverse[slots].reshape(-1).astype(jnp.int32)


def draw_basis_lists(key, part):
    scores = jax.random.randint(jax.random.fold_in(key, 21), (BATCHES, S), 0, 1048576)
    scores = scores * S + jnp.arange(S)[None, :]
    order = jnp.argsort(scores, axis=1)
    return order[:, :K].astype(jnp.int32)


def draw_point_counts(key, part):
    devices_all = N_WIDE * N_NARROW
    levels = jax.random.randint(jax.random.fold_in(key, 31), (devices_all,), 1, 5)
    chosen = jax.random.randint(jax.random.fold_in(key, 32), (), 0, devices_all)
    levels = jnp.where(jnp.arange(devices_all) == chosen, 4, levels)
    limits = PTS * levels // 4
    device_of = jnp.arange(BATCHES) // BATCH_DEV
    batch_of = jnp.arange(BATCHES) % BATCH_DEV
    limit_row = limits[device_of]
    raw = jax.random.randint(jax.random.fold_in(key, 33), (BATCHES,), 0, PTS)
    counts = 1 + raw % limit_row
    return jnp.where(batch_of == 0, limit_row, counts).astype(jnp.int32)


def draw_harmonics(key, part):
    devices_all = N_WIDE * N_NARROW
    device_of = (jnp.arange(BATCHES) // BATCH_DEV).astype(jnp.float32)
    ramp = 1.0 + 2.0 * device_of / max(devices_all - 1, 1)
    base = jnp.clip(jax.random.normal(key, (BATCHES, NL, PTS), jnp.float32), -4.0, 4.0)
    values = base * ramp[:, None, None]
    return values.astype(jnp.bfloat16)


def level_of(own_key, dims, shards, low, top_value):
    gain, own = 1.0, jax.random.fold_in(own_key, 6)
    for position, shards_of in shards:
        steps = jnp.exp(jax.random.uniform(jax.random.fold_in(own, position), (shards_of,), jnp.float32, low / len(shards), top_value / len(shards)))
        gain = gain * jnp.repeat(steps, dims[position] // shards_of).reshape([-1 if axis == position else 1 for axis in range(len(dims))])
    return gain


def normal_values(stream_key, extent, spread, bound, pieces=(), held_as=jnp.bfloat16):
    values = jax.random.normal(stream_key, extent, jnp.float32) * spread
    if len(pieces) > 0:
        values = level_of(stream_key, extent, pieces, -0.22, 0.18) * values
    return jnp.clip(values, min=-bound, max=bound).astype(held_as)


def setup_inputs(seed: int = 0) -> dict:
    keys = jax.random.split(jax.random.key(seed), 9)
    return {
        "density": normal_values(keys[0], (NB * BLK, NB * BLK), 0.001, 0.0059814453, ((0, 8), (1, 4))),
        "block_slot": draw_block_slot(jax.random.fold_in(keys[8], 71), 0),
        "region_blocks": draw_region_blocks(jax.random.fold_in(keys[8], 71), 0),
        "basis_lists": draw_basis_lists(jax.random.fold_in(keys[8], 71), 0),
        "point_counts": draw_point_counts(jax.random.fold_in(keys[8], 71), 0),
        "orbitals": normal_values(keys[5], (BATCHES, K * BLK, PTS), 1.0, 6.0, ((0, 32),)),
        "weights": jnp.clip(jnp.exp(math.log(0.1) - 2.3025851 * jax.random.uniform(keys[6], (BATCHES, PTS), jnp.float32) ** level_of(keys[6], (BATCHES, PTS), ((0, 32),), -0.2, 0.2)), 0.01, 0.1),
        "harmonics": draw_harmonics(jax.random.fold_in(keys[8], 71), 0),
    }


FAR_COEFF = 10.0

def layout_positions(slots):
    col_blocks = NB // N_NARROW
    row_index = slots % N_WIDE * QB + slots // N_WIDE
    col_index = slots % N_NARROW * col_blocks + slots // N_NARROW
    return (row_index, col_index)

def reference(density, block_slot, region_blocks, basis_lists, point_counts, orbitals, weights, harmonics):
    devices_all = N_WIDE * N_NARROW
    slots = block_slot[region_blocks].reshape(devices_all, S)
    row_index, col_index = layout_positions(slots)
    blocks_four = density.reshape(NB, BLK, NB, BLK)
    lists_all = basis_lists.reshape(devices_all, BATCH_DEV, K)
    orbs_all = orbitals.reshape(devices_all, BATCH_DEV, K, BLK, PTS)

    def device_density(packed):
        rows_dev, cols_dev, lists_dev, orbs_dev = packed
        region = blocks_four[rows_dev[:, None], :, cols_dev[None, :], :].astype(jnp.float32)

        def batch_density(inner):
            list_row, orb_rows = inner
            sub_matrix = region[list_row[:, None], list_row[None, :]]
            orb_float = orb_rows.astype(jnp.float32)
            product = jnp.einsum('acij,cjp->aip', sub_matrix, orb_float, precision=lax.Precision.HIGHEST)
            return lax.optimization_barrier(jnp.sum(product * orb_float, axis=(0, 1)))
        return lax.map(batch_density, (lists_dev, orbs_dev))
    dens_pts = lax.map(device_density, (row_index, col_index, lists_all, orbs_all)).reshape(BATCHES, PTS)
    live_mask = jnp.arange(PTS)[None, :] < point_counts[:, None]
    live_weight = jnp.where(live_mask, weights, jnp.float32(0.0))
    harm_float = harmonics.astype(jnp.float32)
    moments = lax.optimization_barrier(jnp.sum((live_weight * dens_pts)[:, None, :] * harm_float, axis=(0, 2)))
    far_field = FAR_COEFF * lax.optimization_barrier(jnp.sum(moments[None, :, None] * harm_float, axis=1)) / math.sqrt(TOTAL_PTS * NL)
    potential = 0.5 * dens_pts - (1.0 + dens_pts * dens_pts) ** (1.0 / 6.0) + far_field
    factor = live_weight * potential
    orb_four = orbitals.reshape(BATCHES, K, BLK, PTS)
    scaled = lax.optimization_barrier((orb_four.astype(jnp.float32) * factor[:, None, None, :]).astype(jnp.bfloat16))
    scaled_all = scaled.reshape(devices_all, BATCH_DEV, K, BLK, PTS)

    def add_device(total, packed):
        rows_dev, cols_dev, lists_dev, scaled_dev, orbs_dev = packed

        def add_batch(partial_h, inner):
            list_row, scaled_rows, orb_rows = inner
            term = jnp.einsum('aip,cjp->acij', scaled_rows.astype(jnp.float32), orb_rows.astype(jnp.float32), precision=lax.Precision.HIGHEST)
            return (partial_h.at[list_row[:, None], list_row[None, :]].add(term), None)
        start = jnp.zeros((S, S, BLK, BLK), jnp.float32)
        partial_h = lax.scan(add_batch, start, (lists_dev, scaled_dev, orbs_dev))[0]
        rounded = lax.optimization_barrier(partial_h.astype(jnp.bfloat16)).astype(jnp.float32)
        return (total.at[rows_dev[:, None], :, cols_dev[None, :], :].add(rounded), None)
    total = jnp.zeros((NB, BLK, NB, BLK), jnp.float32)
    total = lax.scan(add_device, total, (row_index, col_index, lists_all, scaled_all, orbs_all))[0]
    return total.reshape(NB * BLK, NB * BLK)
```

```python
import functools
import math

import jax
import jax.numpy as jnp
from jax import lax
from jax.experimental import pallas as pl
from jax.experimental.pallas import tpu as pltpu
from jax.sharding import PartitionSpec as P

BLK = 128
FAR_COEFF = 10.0
RING = 4
LANES = 128
CHUNK = 512
MESH = pl.DeviceIdType.MESH
VMEM_BYTES = 63 * 1024 * 1024


def ring_device(shift, inner):
    wide = lax.axis_size("wide")
    return (lax.rem(lax.axis_index("wide") + shift * inner + wide, wide), lax.axis_index("narrow"))


def any_device(offset):
    narrow = lax.axis_size("narrow")
    devices = lax.axis_size("wide") * narrow
    mine = lax.axis_index("wide") * narrow + lax.axis_index("narrow")
    other = lax.rem(mine + offset, devices)
    return mine, (other // narrow, other % narrow)


def step_kernel(
    steps,
    inner,
    narrow,
    row_cap,
    col_cap,
    far_scale,
    inv_ref,
    cols_ref,
    counts_ref,
    tile_ref,
    weights_ref,
    dens_ref,
    orb_ref,
    harm_ref,
    out_ref,
    *rest,
):
    raws, rest = rest[:steps], rest[steps:]
    arrs, rest = rest[:steps], rest[steps:]
    (
        chosen,
        tables,
        table,
        even,
        odd,
        phi,
        rows,
        harms,
        rho,
        factor,
        share,
        shares,
        ostage,
        send_sem,
        recv_sem,
        ring_send,
        ring_recv,
        load_sem,
        tile_send,
        tile_recv,
        orb_sem,
        local_sem,
        share_send,
        share_recv,
        out_sem,
    ) = rest
    devices = lax.axis_size("wide") * narrow
    group = inner * narrow
    cap = row_cap * col_cap
    wide_me = lax.axis_index("wide")
    inner_me = wide_me % inner
    ring_me = wide_me // inner
    base = ring_me * inner
    narrow_me = lax.axis_index("narrow")
    mine = inner_me * narrow + narrow_me
    col_blocks = dens_ref.shape[1] // BLK
    row_blocks = dens_ref.shape[0] // BLK
    held = row_blocks * col_blocks
    empty = group * cap
    batches, list_len, _, points = orb_ref.shape
    all_points = batches * points
    slots = narrow * col_cap
    tall = row_cap * BLK
    broad = col_cap * BLK

    def target(place):
        across = lax.rem(inner_me + place // narrow, inner)
        along = lax.rem(narrow_me + place % narrow, narrow)
        return across, along

    def source(place):
        across = lax.rem(inner_me + inner - place // narrow, inner)
        along = lax.rem(narrow_me + narrow - place % narrow, narrow)
        return across, along

    def load_copy(place):
        row, col = place // col_blocks, place % col_blocks
        return pltpu.make_async_copy(
            dens_ref.at[
                pl.ds(pl.multiple_of(row * BLK, BLK), BLK),
                pl.ds(pl.multiple_of(col * BLK, BLK), BLK),
            ],
            raws[0].at[place],
            load_sem.at[place],
        )

    stages = (even, odd)

    def orb_copy(batch, which):
        return pltpu.make_async_copy(
            orb_ref.at[batch], stages[which].at[pl.ds(0, list_len)], orb_sem.at[which]
        )

    def block_copy(step, place):
        across, along = target(place)
        return pltpu.make_async_remote_copy(
            src_ref=chosen.at[step % 2, place],
            dst_ref=arrs[step].at[pl.ds(mine * cap, cap)],
            send_sem=send_sem.at[step, place],
            recv_sem=recv_sem.at[step, place],
            device_id=(base + across, along),
            device_id_type=MESH,
        )

    def ring_copy(step, piece):
        span = pl.ds(piece * col_blocks, col_blocks)
        return pltpu.make_async_remote_copy(
            src_ref=raws[step].at[span],
            dst_ref=raws[step + 1].at[span],
            send_sem=ring_send.at[step, piece],
            recv_sem=ring_recv.at[step, piece],
            device_id=ring_device(1, inner),
            device_id_type=MESH,
        )

    def tile_copy(place):
        across, along = target(place)
        return pltpu.make_async_remote_copy(
            src_ref=tile_ref,
            dst_ref=tables.at[mine],
            send_sem=tile_send.at[place],
            recv_sem=tile_recv.at[place],
            device_id=(base + across, along),
            device_id_type=MESH,
        )

    def share_copy(offset):
        whose, device = any_device(offset)
        return pltpu.make_async_remote_copy(
            src_ref=share,
            dst_ref=shares.at[whose],
            send_sem=share_send.at[offset],
            recv_sem=share_recv.at[offset],
            device_id=device,
            device_id_type=MESH,
        )

    def over(first, last, make, act):
        def body(index, carry):
            act(make(index))
            return carry

        lax.fori_loop(first, last, body, 0)

    start = lambda copy: copy.start()
    wait = lambda copy: copy.wait()
    wait_send = lambda copy: copy.wait_send()
    wait_recv = lambda copy: copy.wait_recv()

    over(0, held, load_copy, start)
    barrier = pltpu.get_barrier_semaphore()

    def greet(offset, carry):
        _, device = any_device(offset)
        pl.semaphore_signal(barrier, inc=1, device_id=device, device_id_type=MESH)
        return carry

    lax.fori_loop(1, devices, greet, 0)
    for which in range(min(2, batches)):
        orb_copy(which, which).start()
    load_harms = pltpu.make_async_copy(harm_ref, harms, local_sem.at[0])
    load_harms.start()
    tables[mine] = tile_ref[...]
    for step in range(steps):
        arrs[step][empty] = jnp.zeros((BLK, BLK), arrs[step].dtype)
    for stage in stages:
        stage[list_len] = jnp.zeros((BLK, points), stage.dtype)
    phi[slots] = jnp.zeros((BLK, all_points), phi.dtype)
    rho[...] = jnp.zeros_like(rho)
    over(0, held, load_copy, wait)
    pl.semaphore_wait(barrier, devices - 1)
    over(1, group, tile_copy, start)

    def pass_on(step):
        for piece in range(row_blocks):
            if step > 0:
                ring_copy(step - 1, piece).wait_recv()
            if step < steps - 1:
                ring_copy(step, piece).start()

    def pick(step, place, put):
        across, along = target(place)
        other = across * narrow + along
        ring = lax.rem(ring_me - step + steps, steps)
        for rr in range(row_cap):
            row = table[other, 0, (ring * inner + inner_me) * row_cap + rr] * col_blocks
            for cr in range(col_cap):
                spot = row + table[other, 1, narrow_me * col_cap + cr]
                put(rr * col_cap + cr, raws[step][spot])

    def send_picks(step):
        def put_own(index, value):
            arrs[step][mine * cap + index] = value

        def body(count, carry):
            place = group - 1 - count

            def put(index, value):
                chosen[step % 2, place, index] = value

            pick(step, place, put)

            @pl.when(count > 0)
            def _():
                block_copy(step, place + 1).start()

            return carry

        lax.fori_loop(0, group - 1, body, 0)
        pick(step, 0, put_own)
        block_copy(step, 1).start()

    def density_piece(step, place):
        across, along = source(place)
        first = (across * narrow + along) * cap
        ring = lax.rem(ring_me - step + steps, steps)
        owner = (ring * inner + across) * row_cap
        block = jnp.concatenate(
            [
                jnp.concatenate(
                    [arrs[step][first + rr * col_cap + cr] for cr in range(col_cap)], axis=1
                )
                for rr in range(row_cap)
            ],
            axis=0,
        )
        spots = [cols_ref[owner + rr] for rr in range(row_cap)]
        down = pl.ds(along * col_cap, col_cap)

        def chunk(index, carry):
            span = pl.ds(pl.multiple_of(index * CHUNK, CHUNK), CHUNK)
            wave = phi[down, :, span].reshape(broad, CHUNK)
            product = jnp.dot(block, wave, preferred_element_type=jnp.float32)
            total = rho[:, span]
            for rr in range(row_cap):
                mate = phi[spots[rr], :, span]
                part = product[rr * BLK : (rr + 1) * BLK] * mate.astype(jnp.float32)
                total += jnp.sum(part.reshape(BLK // 8, 8, CHUNK), axis=0)
            rho[:, span] = total
            return carry

        lax.fori_loop(0, all_points // CHUNK, chunk, 0)

    def density_step(step):
        density_piece(step, 0)

        def body(count, carry):
            place = group - 1 - count
            block_copy(step, place).wait_recv()
            density_piece(step, place)
            return carry

        lax.fori_loop(0, group - 1, body, 0)

    def build(batch, which):
        orb_copy(batch, which).wait()
        across = pl.ds(pl.multiple_of(batch * points, points), points)
        for slot in range(slots):
            phi[slot, :, across] = stages[which][inv_ref[batch, slot]]

        @pl.when(batch + 2 < batches)
        def _():
            orb_copy(batch + 2, which).start()

    def build_pair(pair, carry):
        for which in range(2):
            build(pair * 2 + which, which)
        return carry

    pass_on(0)
    over(1, group, tile_copy, wait)
    to_table = pltpu.make_async_copy(tables, table, local_sem.at[1])
    to_table.start()
    to_table.wait()
    send_picks(0)
    lax.fori_loop(0, batches // 2, build_pair, 0)
    if batches % 2:
        build(batches - 1, 0)
    for step in range(1, steps + 1):
        if step < steps:
            pass_on(step)
            if step >= 2:
                over(1, group, functools.partial(block_copy, step - 2), wait_send)
            send_picks(step)
        density_step(step - 1)

    load_harms.wait()

    def live_row(batch):
        point = lax.broadcasted_iota(jnp.int32, (1, points), 1)
        return jnp.where(
            point < counts_ref[batch], weights_ref[pl.ds(batch, 1), :], jnp.float32(0.0)
        )

    components = harms.shape[1]
    moment = jnp.zeros((components, points), jnp.float32)
    for batch in range(batches):
        across = slice(batch * points, (batch + 1) * points)
        dens = jnp.sum(rho[:, across], axis=0, keepdims=True)
        rho[0:1, across] = dens
        moment += harms[batch].astype(jnp.float32) * (live_row(batch) * dens)
    diagonal = lax.broadcasted_iota(jnp.int32, (components, LANES), 0) == lax.broadcasted_iota(
        jnp.int32, (components, LANES), 1
    )
    summed = jnp.sum(moment, axis=1, keepdims=True)
    line = jnp.sum(jnp.where(diagonal, summed, 0.0), axis=0, keepdims=True)
    share[...] = jnp.broadcast_to(line, share.shape)
    whose, _ = any_device(0)
    shares[whose] = jnp.broadcast_to(line, share.shape)
    for step in range(steps - 1):
        over(0, row_blocks, functools.partial(ring_copy, step), wait_send)
    for step in range(max(0, steps - 2), steps):
        over(1, group, functools.partial(block_copy, step), wait_send)
    over(1, devices, share_copy, start)
    over(1, devices, share_copy, wait)
    line = jnp.sum(shares[...], axis=0)[0:1]
    total_moment = jnp.sum(jnp.where(diagonal, line, 0.0), axis=1, keepdims=True)
    for batch in range(batches):
        across = slice(batch * points, (batch + 1) * points)
        dens = rho[0:1, across]
        far = FAR_COEFF * jnp.sum(
            total_moment * harms[batch].astype(jnp.float32), axis=0, keepdims=True
        )
        sixth = jnp.exp(jnp.log(1.0 + dens * dens) * (1.0 / 6.0))
        potential = 0.5 * dens - sixth + far / far_scale
        factor[:, across] = jnp.broadcast_to(live_row(batch) * potential, (8, points))

    def scale_rows(step, across):
        ring = lax.rem(ring_me - 1 - step + 2 * steps, steps)
        owner = (ring * inner + across) * row_cap
        spots = [cols_ref[owner + rr] for rr in range(row_cap)]

        def chunk(index, carry):
            span = pl.ds(pl.multiple_of(index * CHUNK, CHUNK), CHUNK)
            for rr in range(row_cap):
                mate = phi[spots[rr], :, span]
                scaled = mate.astype(jnp.float32) * factor[0:1, span]
                rows[rr * BLK : (rr + 1) * BLK, span] = scaled.astype(rows.dtype)
            return carry

        lax.fori_loop(0, all_points // CHUNK, chunk, 0)

    def integral_piece(along, put):
        down = pl.ds(along * col_cap, col_cap)
        term = lax.dot_general(
            rows[...],
            phi[down].reshape(broad, all_points),
            (((1,), (1,)), ((), ())),
            preferred_element_type=jnp.float32,
        )
        for rr in range(row_cap):
            for cr in range(col_cap):
                value = term[rr * BLK : (rr + 1) * BLK, cr * BLK : (cr + 1) * BLK]
                put(rr * col_cap + cr, value.astype(chosen.dtype))

    def send_integrals(step):
        if step >= 2:
            over(1, group, functools.partial(block_copy, step - 2), wait_send)

        def piece(place):
            _, along = target(place)

            def put(index, value):
                chosen[step % 2, place, index] = value

            integral_piece(along, put)

            @pl.when(place < group - 1)
            def _():
                block_copy(step, place + 1).start()

        def far_rows(count, carry):
            shift = inner - 1 - count
            scale_rows(step, lax.rem(inner_me + shift, inner))

            def body(index, inner_carry):
                piece(shift * narrow + narrow - 1 - index)
                return inner_carry

            lax.fori_loop(0, narrow, body, 0)
            return carry

        lax.fori_loop(0, inner - 1, far_rows, 0)
        scale_rows(step, inner_me)

        def near(index, carry):
            piece(narrow - 1 - index)
            return carry

        lax.fori_loop(0, narrow - 1, near, 0)

        def put_own(index, value):
            arrs[step][mine * cap + index] = value

        integral_piece(narrow_me, put_own)
        block_copy(step, 1).start()

    def out_copy(piece):
        return pltpu.make_async_copy(
            ostage.at[piece % 2],
            out_ref.at[pl.ds(pl.multiple_of(piece * BLK, BLK), BLK)],
            out_sem.at[piece % 2],
        )

    def add_up(step):
        last = step == steps - 1
        ring = lax.rem(ring_me - 1 - step + 2 * steps, steps)
        over(1, group, functools.partial(block_copy, step), wait_recv)
        for piece in range(row_blocks):
            if step > 0:
                ring_copy(step - 1, piece).wait_recv()
            if last and piece >= 2:
                out_copy(piece - 2).wait()
            bases = [
                table[one, 2, (ring * inner + inner_me) * row_blocks + piece] + one * cap
                for one in range(group)
            ]

            def add_block(block, carry, piece=piece, bases=bases):
                spot = piece * col_blocks + block
                if step > 0:
                    total = raws[step][spot].astype(jnp.float32)
                else:
                    total = jnp.zeros((BLK, BLK), jnp.float32)
                for one in range(group):
                    col = table[one, 3, narrow_me * col_blocks + block]
                    place = jnp.minimum(bases[one] + col, empty)
                    total += arrs[step][place].astype(jnp.float32)
                if last:
                    across = pl.ds(pl.multiple_of(block * BLK, BLK), BLK)
                    ostage[piece % 2, :, across] = total
                else:
                    raws[step][spot] = total.astype(raws[step].dtype)
                return carry

            lax.fori_loop(0, col_blocks, add_block, 0)
            if last:
                out_copy(piece).start()
            elif piece > 0:
                ring_copy(step, piece - 1).start()
        if not last:
            ring_copy(step, row_blocks - 1).start()
        else:
            for piece in range(max(0, row_blocks - 2), row_blocks):
                out_copy(piece).wait()

    send_integrals(0)
    if steps > 1:
        send_integrals(1)
    for step in range(steps):
        add_up(step)
        if step + 2 < steps:
            send_integrals(step + 2)
    for step in range(max(0, steps - 2), steps):
        over(1, group, functools.partial(block_copy, step), wait_send)
    for step in range(steps - 1):
        over(0, row_blocks, functools.partial(ring_copy, step), wait_send)


def whole_step(inv, cols, counts, tile, weights, dens, orbitals, harmonics, steps, inner, narrow, caps, far_scale):
    row_cap, col_cap = caps
    group = inner * narrow
    cap = row_cap * col_cap
    devices = steps * group
    ring_sems = max(1, steps - 1)
    row_blocks, col_blocks = dens.shape[0] // BLK, dens.shape[1] // BLK
    held = row_blocks * col_blocks
    batches, list_len, _, points = orbitals.shape
    all_points = batches * points
    components = harmonics.shape[1]
    slots = narrow * col_cap
    vmem = pl.BlockSpec(memory_space=pltpu.VMEM)
    smem = pl.BlockSpec(memory_space=pltpu.SMEM)
    anywhere = pl.BlockSpec(memory_space=pl.ANY)
    dma = pltpu.SemaphoreType.DMA
    return pl.pallas_call(
        functools.partial(step_kernel, steps, inner, narrow, row_cap, col_cap, far_scale),
        out_shape=jax.ShapeDtypeStruct(dens.shape, jnp.float32),
        in_specs=[smem] * 3 + [vmem] * 2 + [anywhere] * 3,
        out_specs=anywhere,
        scratch_shapes=[pltpu.VMEM((held, BLK, BLK), dens.dtype)] * steps
        + [pltpu.VMEM((group * cap + 1, BLK, BLK), dens.dtype)] * steps
        + [
            pltpu.VMEM((2, group, cap, BLK, BLK), dens.dtype),
            pltpu.VMEM((group,) + tile.shape, tile.dtype),
            pltpu.SMEM((group,) + tile.shape, tile.dtype),
            pltpu.VMEM((list_len + 1, BLK, points), orbitals.dtype),
            pltpu.VMEM((list_len + 1, BLK, points), orbitals.dtype),
            pltpu.VMEM((slots + 1, BLK, all_points), orbitals.dtype),
            pltpu.VMEM((row_cap * BLK, all_points), orbitals.dtype),
            pltpu.VMEM(harmonics.shape, harmonics.dtype),
            pltpu.VMEM((8, all_points), jnp.float32),
            pltpu.VMEM((8, all_points), jnp.float32),
            pltpu.VMEM((8, LANES), jnp.float32),
            pltpu.VMEM((devices, 8, LANES), jnp.float32),
            pltpu.VMEM((2, BLK, dens.shape[1]), jnp.float32),
            dma((steps, group)),
            dma((steps, group)),
            dma((ring_sems, row_blocks)),
            dma((ring_sems, row_blocks)),
            dma((held,)),
            dma((group,)),
            dma((group,)),
            dma((2,)),
            dma((2,)),
            dma((devices,)),
            dma((devices,)),
            dma((2,)),
        ],
        compiler_params=pltpu.CompilerParams(
            collective_id=1, has_side_effects=True, vmem_limit_bytes=VMEM_BYTES
        ),
        name="grid_step",
    )(inv, cols, counts, tile, weights, dens, orbitals, harmonics)


def rank_among(keys):
    count = keys.shape[0]
    order = jnp.arange(count)
    same = (keys[:, None] == keys[None, :]) & (order[None, :] < order[:, None])
    return jnp.sum(same.astype(jnp.int32), axis=1)


def spread(positions, values, size):
    hit = positions[None, :] == jnp.arange(size)[:, None]
    return jnp.sum(jnp.where(hit, values[None, :], 0), axis=1)


def per_device(
    region, density, block_slot, region_blocks, basis_lists, point_counts, orbitals, weights, harmonics
):
    wide = lax.axis_size("wide")
    narrow = lax.axis_size("narrow")
    devices = wide * narrow
    steps = math.gcd(wide, RING)
    inner = wide // steps
    row_cap = max(1, region // wide)
    col_cap = region // narrow

    known = block_slot.shape[0]
    hit = region_blocks[:, None] == jnp.arange(known)[None, :]
    slots = jnp.sum(jnp.where(hit, block_slot[None, :], 0), axis=1)
    row_owner, row_local = slots % wide, slots // wide
    col_owner, col_local = slots % narrow, slots // narrow
    row_rank, col_rank = rank_among(row_owner), rank_among(col_owner)
    row_place = row_owner * row_cap + row_rank
    col_place = col_owner * col_cap + col_rank
    row_table = spread(row_place, row_local, LANES)
    col_table = spread(col_place, col_local, LANES)
    far = 1 << 20
    row_blocks = density.shape[0] // BLK
    col_blocks = density.shape[1] // BLK
    row_back = far + spread(
        row_owner * row_blocks + row_local, row_rank * col_cap - far, LANES
    )
    col_back = far + spread(col_owner * col_blocks + col_local, col_rank - far, LANES)
    tile = jnp.stack([row_table, col_table, row_back, col_back] * 2)
    none = region
    cols = none + spread(row_place, col_place - none, wide * row_cap)
    list_len = basis_lists.shape[1]
    owner_of = spread(col_place, jnp.arange(region), narrow * col_cap)
    listed = basis_lists[:, :, None] == owner_of[None, None, :]
    order = jnp.arange(list_len)[None, :, None]
    inv = list_len + jnp.sum(jnp.where(listed, order - list_len, 0), axis=1)

    components = harmonics.shape[1]
    batches, _, points = orbitals.shape
    total_points = batches * points * devices
    return whole_step(
        inv,
        cols,
        point_counts,
        tile,
        weights,
        density,
        orbitals.reshape(batches, list_len, BLK, points),
        harmonics,
        steps,
        inner,
        narrow,
        (row_cap, col_cap),
        math.sqrt(total_points * components),
    )


def solution(mesh):
    devices = mesh.shape["wide"] * mesh.shape["narrow"]

    def whole(density, block_slot, region_blocks, *others):
        region = region_blocks.shape[0] // devices
        in_specs = (
            P("wide", "narrow"),
            P(),
            P(("wide", "narrow")),
            P(("wide", "narrow"), None),
            P(("wide", "narrow")),
            P(("wide", "narrow"), None, None),
            P(("wide", "narrow"), None),
            P(("wide", "narrow"), None, None),
        )
        mapped = jax.shard_map(
            functools.partial(per_device, region),
            mesh=mesh,
            in_specs=in_specs,
            out_specs=P("wide", "narrow"),
            check_vma=False,
        )
        return mapped(density, block_slot, region_blocks, *others)

    return whole
```

```python
import functools
import math

import jax
import jax.numpy as jnp
from jax import lax
from jax.experimental import pallas as pl
from jax.experimental.pallas import tpu as pltpu
from jax.sharding import PartitionSpec as P

BLK = 128
FAR_COEFF = 10.0
RING = 4
LANES = 128
CHUNK = 512
HALVES = 2
HALF = BLK // HALVES
MESH = pl.DeviceIdType.MESH
VMEM_BYTES = 63 * 1024 * 1024


def ring_device(shift, inner):
    wide = lax.axis_size("wide")
    return (lax.rem(lax.axis_index("wide") + shift * inner + wide, wide), lax.axis_index("narrow"))


def any_device(offset):
    narrow = lax.axis_size("narrow")
    devices = lax.axis_size("wide") * narrow
    mine = lax.axis_index("wide") * narrow + lax.axis_index("narrow")
    other = lax.rem(mine + offset, devices)
    return mine, (other // narrow, other % narrow)


def step_kernel(
    steps,
    inner,
    narrow,
    row_cap,
    col_cap,
    far_scale,
    slot_ref,
    region_ref,
    lists_ref,
    counts_ref,
    weights_ref,
    dens_ref,
    orb_ref,
    harm_ref,
    out_ref,
    *rest,
):
    count = steps * HALVES
    raws = [rest[step * HALVES : (step + 1) * HALVES] for step in range(steps)]
    arrs = [rest[count + step * HALVES : count + (step + 1) * HALVES] for step in range(steps)]
    rest = rest[2 * count :]
    (
        chosen,
        slot_of,
        region_of,
        lists,
        counts,
        weights,
        places,
        tile,
        own_inv,
        inv,
        tables,
        table,
        even,
        odd,
        phi,
        rows,
        harms,
        rho,
        factor,
        share,
        shares,
        ostage,
        send_sem,
        recv_sem,
        ring_send,
        ring_recv,
        load_sem,
        tile_send,
        tile_recv,
        orb_sem,
        local_sem,
        int_sem,
        share_send,
        share_recv,
        out_sem,
    ) = rest
    devices = lax.axis_size("wide") * narrow
    group = inner * narrow
    cap = row_cap * col_cap
    wide_me = lax.axis_index("wide")
    inner_me = wide_me % inner
    ring_me = wide_me // inner
    base = ring_me * inner
    narrow_me = lax.axis_index("narrow")
    mine = inner_me * narrow + narrow_me
    col_blocks = dens_ref.shape[1] // BLK
    row_blocks = dens_ref.shape[0] // BLK
    held = row_blocks * col_blocks
    empty = group * cap
    batches, list_len, _, points = orb_ref.shape
    all_points = batches * points
    slots = narrow * col_cap
    tall = row_cap * BLK
    broad = col_cap * BLK

    def target(place):
        across = lax.rem(inner_me + place // narrow, inner)
        along = lax.rem(narrow_me + place % narrow, narrow)
        return across, along

    def source(place):
        across = lax.rem(inner_me + inner - place // narrow, inner)
        along = lax.rem(narrow_me + narrow - place % narrow, narrow)
        return across, along

    def load_copy(half, place):
        row, col = place // col_blocks, place % col_blocks
        return pltpu.make_async_copy(
            dens_ref.at[
                pl.ds(pl.multiple_of(row * BLK + half * HALF, HALF), HALF),
                pl.ds(pl.multiple_of(col * BLK, BLK), BLK),
            ],
            raws[0][half].at[place],
            load_sem.at[half],
        )

    def loaded(half):
        pltpu.make_async_copy(raws[0][half], raws[0][half], load_sem.at[half]).wait()

    stages = (even, odd)

    def orb_copy(batch, which):
        return pltpu.make_async_copy(
            orb_ref.at[batch], stages[which].at[pl.ds(0, list_len)], orb_sem.at[which]
        )

    def block_copy(step, half, place):
        across, along = target(place)
        return pltpu.make_async_remote_copy(
            src_ref=chosen.at[step % 2, half, place],
            dst_ref=arrs[step][half].at[pl.ds(mine * cap, cap)],
            send_sem=send_sem.at[step, half, place],
            recv_sem=recv_sem.at[step, half, place],
            device_id=(base + across, along),
            device_id_type=MESH,
        )

    def ring_copy(step, half, piece):
        span = pl.ds(piece * col_blocks, col_blocks)
        return pltpu.make_async_remote_copy(
            src_ref=raws[step][half].at[span],
            dst_ref=raws[step + 1][half].at[span],
            send_sem=ring_send.at[step, half, piece],
            recv_sem=ring_recv.at[step, half, piece],
            device_id=ring_device(1, inner),
            device_id_type=MESH,
        )

    def tile_copy(place):
        across, along = target(place)
        return pltpu.make_async_remote_copy(
            src_ref=tile,
            dst_ref=tables.at[mine],
            send_sem=tile_send.at[place],
            recv_sem=tile_recv.at[place],
            device_id=(base + across, along),
            device_id_type=MESH,
        )

    def share_copy(offset):
        whose, device = any_device(offset)
        return pltpu.make_async_remote_copy(
            src_ref=share,
            dst_ref=shares.at[whose],
            send_sem=share_send.at[offset],
            recv_sem=share_recv.at[offset],
            device_id=device,
            device_id_type=MESH,
        )

    def over(first, last, make, act):
        def body(index, carry):
            act(make(index))
            return carry

        lax.fori_loop(first, last, body, 0)

    start = lambda copy: copy.start()
    wait = lambda copy: copy.wait()
    wait_send = lambda copy: copy.wait_send()
    wait_recv = lambda copy: copy.wait_recv()

    barrier = pltpu.get_barrier_semaphore()

    def greet(place, carry):
        across, along = target(place)
        pl.semaphore_signal(barrier, inc=1, device_id=(base + across, along), device_id_type=MESH)
        return carry

    lax.fori_loop(1, group, greet, 0)
    if steps > 1:
        for shift in (1, -1):
            pl.semaphore_signal(
                barrier, inc=1, device_id=ring_device(shift, inner), device_id_type=MESH
            )
    integers = [
        pltpu.make_async_copy(given, held_in, int_sem.at[index])
        for index, (given, held_in) in enumerate(
            ((slot_ref, slot_of), (region_ref, region_of), (lists_ref, lists), (counts_ref, counts))
        )
    ]
    for copy in integers:
        copy.start()
    for half in range(HALVES):
        over(0, held, functools.partial(load_copy, half), start)
    for which in range(min(2, batches)):
        orb_copy(which, which).start()
    load_harms = pltpu.make_async_copy(harm_ref, harms, local_sem.at[0])
    load_harms.start()
    load_weights = pltpu.make_async_copy(weights_ref, weights, local_sem.at[2])
    load_weights.start()
    for step in range(steps):
        for half in range(HALVES):
            arrs[step][half][empty] = jnp.zeros((HALF, BLK), chosen.dtype)
    for stage in stages:
        stage[list_len] = jnp.zeros((BLK, points), stage.dtype)
    phi[slots] = jnp.zeros((BLK, all_points), phi.dtype)
    rho[...] = jnp.zeros_like(rho)
    for copy in integers:
        copy.wait()

    region = region_of.shape[0]
    wide = lax.axis_size("wide")
    named = [slot_of[region_of[spot]] for spot in range(region)]
    lane = lax.broadcasted_iota(jnp.int32, (8, LANES), 1)
    line = lax.broadcasted_iota(jnp.int32, (8, LANES), 0)
    far = 1 << 20
    row_table = jnp.zeros((8, LANES), jnp.int32)
    col_table = jnp.zeros((8, LANES), jnp.int32)
    row_back = jnp.full((8, LANES), far, jnp.int32)
    col_back = jnp.full((8, LANES), far, jnp.int32)
    cross = jnp.full((8, LANES), slots, jnp.int32)
    row_owners = [lax.rem(slot, wide) for slot in named]
    col_owners = [lax.rem(slot, narrow) for slot in named]
    for spot in range(region):
        row_local, col_local = named[spot] // wide, named[spot] // narrow
        row_rank, col_rank = jnp.int32(0), jnp.int32(0)
        for earlier in range(spot):
            row_rank += (row_owners[earlier] == row_owners[spot]).astype(jnp.int32)
            col_rank += (col_owners[earlier] == col_owners[spot]).astype(jnp.int32)
        row_place = row_owners[spot] * row_cap + row_rank
        col_place = col_owners[spot] * col_cap + col_rank
        places[spot] = col_place
        row_table = jnp.where(lane == row_place, row_local, row_table)
        col_table = jnp.where(lane == col_place, col_local, col_table)
        row_back = jnp.where(
            lane == row_owners[spot] * row_blocks + row_local, row_rank * col_cap, row_back
        )
        col_back = jnp.where(lane == col_owners[spot] * col_blocks + col_local, col_rank, col_back)
        cross = jnp.where(lane == row_place, col_place, cross)
    index_tile = jnp.where(line == 0, row_table, cross)
    index_tile = jnp.where(line == 1, col_table, index_tile)
    index_tile = jnp.where(line == 2, row_back, index_tile)
    index_tile = jnp.where(line == 3, col_back, index_tile)
    tile[...] = index_tile
    tables[mine] = index_tile
    pl.semaphore_wait(barrier, group - 1 + (2 if steps > 1 else 0))
    over(1, group, tile_copy, start)

    def pass_on(step, half):
        for piece in range(row_blocks):
            if step > 0:
                ring_copy(step - 1, half, piece).wait_recv()
            if step < steps - 1:
                ring_copy(step, half, piece).start()

    def pick(step, half, place, put):
        across, along = target(place)
        other = across * narrow + along
        ring = lax.rem(ring_me - step + steps, steps)
        for rr in range(row_cap):
            row = table[other, 0, (ring * inner + inner_me) * row_cap + rr] * col_blocks
            for cr in range(col_cap):
                spot = row + table[other, 1, narrow_me * col_cap + cr]
                put(rr * col_cap + cr, raws[step][half][spot])

    def send_picks(step, half):
        if step >= 2:
            over(1, group, functools.partial(block_copy, step - 2, half), wait_send)

        def put_own(index, value):
            arrs[step][half][mine * cap + index] = value

        def body(count, carry):
            place = group - 1 - count

            def put(index, value):
                chosen[step % 2, half, place, index] = value

            pick(step, half, place, put)

            @pl.when(count > 0)
            def _():
                block_copy(step, half, place + 1).start()

            return carry

        lax.fori_loop(0, group - 1, body, 0)
        pick(step, half, 0, put_own)
        block_copy(step, half, 1).start()

    def density_piece(step, halves, place):
        across, along = source(place)
        first = (across * narrow + along) * cap
        ring = lax.rem(ring_me - step + steps, steps)
        owner = (ring * inner + across) * row_cap
        block = jnp.concatenate(
            [
                jnp.concatenate(
                    [arrs[step][half][first + rr * col_cap + cr] for cr in range(col_cap)], axis=1
                )
                for rr in range(row_cap)
                for half in halves
            ],
            axis=0,
        )
        spots = [table[mine, 4, owner + rr] for rr in range(row_cap)]
        down = pl.ds(along * col_cap, col_cap)
        low, size = halves[0] * HALF, len(halves) * HALF

        def chunk(index, carry):
            span = pl.ds(pl.multiple_of(index * CHUNK, CHUNK), CHUNK)
            wave = phi[down, :, span].reshape(broad, CHUNK)
            product = jnp.dot(block, wave, preferred_element_type=jnp.float32)
            total = rho[:, span]
            for rr in range(row_cap):
                mate = phi[spots[rr], low : low + size, span]
                part = product[rr * size : (rr + 1) * size] * mate.astype(jnp.float32)
                total += jnp.sum(part.reshape(size // 8, 8, CHUNK), axis=0)
            rho[:, span] = total
            return carry

        lax.fori_loop(0, all_points // CHUNK, chunk, 0, unroll=True)

    def density_pieces(step, halves, first, last):
        def body(count, carry):
            place = group - 1 - count
            for half in halves:
                block_copy(step, half, place).wait_recv()
            density_piece(step, halves, place)
            return carry

        lax.fori_loop(first, last, body, 0)

    def build(batch, which):
        orb_copy(batch, which).wait()
        across = pl.ds(pl.multiple_of(batch * points, points), points)
        for slot in range(slots):
            phi[slot, :, across] = stages[which][inv[batch, slot]]

        @pl.when(batch + 2 < batches)
        def _():
            orb_copy(batch + 2, which).start()

    def build_pair(pair, carry):
        for which in range(2):
            build(pair * 2 + which, which)
        return carry

    both = tuple(range(HALVES))
    for half in both:
        loaded(half)
        pass_on(0, half)
    over(1, group, tile_copy, wait)
    to_table = pltpu.make_async_copy(tables, table, local_sem.at[1])
    to_table.start()
    to_table.wait()
    for half in both:
        send_picks(0, half)
    for batch in range(batches):
        found = jnp.full((8, LANES), list_len, jnp.int32)
        for spot in range(list_len):
            found = jnp.where(lane == places[lists[batch, spot]], spot, found)
        own_inv[batch : batch + 1, :] = found[0:1]
    to_inv = pltpu.make_async_copy(own_inv, inv, local_sem.at[3])
    to_inv.start()
    to_inv.wait()
    lax.fori_loop(0, batches // 2, build_pair, 0)
    if batches % 2:
        build(batches - 1, 0)
    middle = group // 2
    for step in range(1, steps):
        pass_on(step, 0)
        send_picks(step, 0)
        density_pieces(step - 1, both, 0, middle)
        pass_on(step, 1)
        send_picks(step, 1)
        density_pieces(step - 1, both, middle, group - 1)
        density_piece(step - 1, both, 0)
    for half in both:
        density_piece(steps - 1, (half,), 0)
        density_pieces(steps - 1, (half,), 0, group - 1)

    load_harms.wait()
    load_weights.wait()

    def live_row(batch):
        point = lax.broadcasted_iota(jnp.int32, (1, points), 1)
        return jnp.where(
            point < counts[batch], weights[pl.ds(batch, 1), :], jnp.float32(0.0)
        )

    components = harms.shape[1]
    moment = jnp.zeros((components, points), jnp.float32)
    for batch in range(batches):
        across = slice(batch * points, (batch + 1) * points)
        dens = jnp.sum(rho[:, across], axis=0, keepdims=True)
        rho[0:1, across] = dens
        moment += harms[batch].astype(jnp.float32) * (live_row(batch) * dens)
    diagonal = lax.broadcasted_iota(jnp.int32, (components, LANES), 0) == lax.broadcasted_iota(
        jnp.int32, (components, LANES), 1
    )
    summed = jnp.sum(moment, axis=1, keepdims=True)
    line = jnp.sum(jnp.where(diagonal, summed, 0.0), axis=0, keepdims=True)
    share[...] = jnp.broadcast_to(line, share.shape)
    whose, _ = any_device(0)
    shares[whose] = jnp.broadcast_to(line, share.shape)
    for half in both:
        for step in range(steps - 1):
            over(0, row_blocks, functools.partial(ring_copy, step, half), wait_send)
        for step in range(max(0, steps - 2), steps):
            over(1, group, functools.partial(block_copy, step, half), wait_send)
    over(1, devices, share_copy, start)
    over(1, devices, share_copy, wait)
    line = jnp.sum(shares[...], axis=0)[0:1]
    total_moment = jnp.sum(jnp.where(diagonal, line, 0.0), axis=1, keepdims=True)
    for batch in range(batches):
        across = slice(batch * points, (batch + 1) * points)
        dens = rho[0:1, across]
        far = FAR_COEFF * jnp.sum(
            total_moment * harms[batch].astype(jnp.float32), axis=0, keepdims=True
        )
        sixth = jnp.exp(jnp.log(1.0 + dens * dens) * (1.0 / 6.0))
        potential = 0.5 * dens - sixth + far / far_scale
        factor[:, across] = jnp.broadcast_to(live_row(batch) * potential, (8, points))

    def scale_rows(step, across):
        ring = lax.rem(ring_me - 1 - step + 2 * steps, steps)
        owner = (ring * inner + across) * row_cap
        spots = [table[mine, 4, owner + rr] for rr in range(row_cap)]

        def chunk(index, carry):
            span = pl.ds(pl.multiple_of(index * CHUNK, CHUNK), CHUNK)
            for rr in range(row_cap):
                mate = phi[spots[rr], :, span]
                scaled = mate.astype(jnp.float32) * factor[0:1, span]
                rows[rr * BLK : (rr + 1) * BLK, span] = scaled.astype(rows.dtype)
            return carry

        lax.fori_loop(0, all_points // CHUNK, chunk, 0)

    def integral_piece(along, put):
        down = pl.ds(along * col_cap, col_cap)
        term = lax.dot_general(
            rows[...],
            phi[down].reshape(broad, all_points),
            (((1,), (1,)), ((), ())),
            preferred_element_type=jnp.float32,
        )
        for rr in range(row_cap):
            for cr in range(col_cap):
                value = term[rr * BLK : (rr + 1) * BLK, cr * BLK : (cr + 1) * BLK]
                put(rr * col_cap + cr, value.astype(chosen.dtype))

    def send_integrals(step):
        if step >= 2:
            for half in both:
                over(1, group, functools.partial(block_copy, step - 2, half), wait_send)

        def piece(place):
            _, along = target(place)

            def put(index, value):
                for half in both:
                    chosen[step % 2, half, place, index] = value[half * HALF : (half + 1) * HALF]

            integral_piece(along, put)

            @pl.when(place < group - 1)
            def _():
                block_copy(step, 0, place + 1).start()

        def far_rows(count, carry):
            shift = inner - 1 - count
            scale_rows(step, lax.rem(inner_me + shift, inner))

            def body(index, inner_carry):
                piece(shift * narrow + narrow - 1 - index)
                return inner_carry

            lax.fori_loop(0, narrow, body, 0)
            return carry

        lax.fori_loop(0, inner - 1, far_rows, 0)
        scale_rows(step, inner_me)

        def near(index, carry):
            piece(narrow - 1 - index)
            return carry

        lax.fori_loop(0, narrow - 1, near, 0)

        def put_own(index, value):
            for half in both:
                arrs[step][half][mine * cap + index] = value[half * HALF : (half + 1) * HALF]

        integral_piece(narrow_me, put_own)
        block_copy(step, 0, 1).start()

        def later(count, carry):
            block_copy(step, 1, group - 1 - count).start()
            return carry

        lax.fori_loop(0, group - 1, later, 0)

    def out_copy(half, piece):
        first = pl.multiple_of(piece * BLK + half * HALF, HALF)
        return pltpu.make_async_copy(
            ostage.at[piece % 2], out_ref.at[pl.ds(first, HALF)], out_sem.at[piece % 2]
        )

    def add_up(step, half):
        last = step == steps - 1
        ring = lax.rem(ring_me - 1 - step + 2 * steps, steps)
        over(1, group, functools.partial(block_copy, step, half), wait_recv)
        for piece in range(row_blocks):
            if step > 0:
                ring_copy(step - 1, half, piece).wait_recv()
            if last and piece >= 2:
                out_copy(half, piece - 2).wait()
            bases = [
                table[one, 2, (ring * inner + inner_me) * row_blocks + piece] + one * cap
                for one in range(group)
            ]

            def add_block(block, carry, piece=piece, bases=bases):
                spot = piece * col_blocks + block
                if step > 0:
                    total = raws[step][half][spot].astype(jnp.float32)
                else:
                    total = jnp.zeros((HALF, BLK), jnp.float32)
                for one in range(group):
                    col = table[one, 3, narrow_me * col_blocks + block]
                    place = jnp.minimum(bases[one] + col, empty)
                    total += arrs[step][half][place].astype(jnp.float32)
                if last:
                    across = pl.ds(pl.multiple_of(block * BLK, BLK), BLK)
                    ostage[piece % 2, :, across] = total
                else:
                    raws[step][half][spot] = total.astype(chosen.dtype)
                return carry

            lax.fori_loop(0, col_blocks, add_block, 0)
            if last:
                out_copy(half, piece).start()
            elif piece > 0:
                ring_copy(step, half, piece - 1).start()
        if not last:
            ring_copy(step, half, row_blocks - 1).start()
        else:
            for piece in range(max(0, row_blocks - 2), row_blocks):
                out_copy(half, piece).wait()

    send_integrals(0)
    for step in range(steps):
        add_up(step, 0)
        if step + 1 < steps:
            send_integrals(step + 1)
        add_up(step, 1)
    for half in both:
        for step in range(max(0, steps - 2), steps):
            over(1, group, functools.partial(block_copy, step, half), wait_send)
        for step in range(steps - 1):
            over(0, row_blocks, functools.partial(ring_copy, step, half), wait_send)


def whole_step(
    block_slot, region_blocks, lists, counts, weights, dens, orbitals, harmonics, steps, inner, narrow, caps, far_scale
):
    row_cap, col_cap = caps
    group = inner * narrow
    cap = row_cap * col_cap
    devices = steps * group
    ring_sems = max(1, steps - 1)
    row_blocks, col_blocks = dens.shape[0] // BLK, dens.shape[1] // BLK
    held = row_blocks * col_blocks
    batches, list_len, _, points = orbitals.shape
    all_points = batches * points
    components = harmonics.shape[1]
    slots = narrow * col_cap
    ints = jnp.int32
    anywhere = pl.BlockSpec(memory_space=pl.ANY)
    dma = pltpu.SemaphoreType.DMA
    return pl.pallas_call(
        functools.partial(step_kernel, steps, inner, narrow, row_cap, col_cap, far_scale),
        out_shape=jax.ShapeDtypeStruct(dens.shape, jnp.float32),
        in_specs=[anywhere] * 8,
        out_specs=anywhere,
        scratch_shapes=[pltpu.VMEM((held, HALF, BLK), dens.dtype)] * (steps * HALVES)
        + [pltpu.VMEM((group * cap + 1, HALF, BLK), dens.dtype)] * (steps * HALVES)
        + [
            pltpu.VMEM((2, HALVES, group, cap, HALF, BLK), dens.dtype),
            pltpu.SMEM(block_slot.shape, ints),
            pltpu.SMEM(region_blocks.shape, ints),
            pltpu.SMEM(lists.shape, ints),
            pltpu.SMEM(counts.shape, ints),
            pltpu.VMEM(weights.shape, weights.dtype),
            pltpu.SMEM(region_blocks.shape, ints),
            pltpu.VMEM((8, LANES), ints),
            pltpu.VMEM((-(-batches // 8) * 8, LANES), ints),
            pltpu.SMEM((-(-batches // 8) * 8, LANES), ints),
            pltpu.VMEM((group, 8, LANES), ints),
            pltpu.SMEM((group, 8, LANES), ints),
            pltpu.VMEM((list_len + 1, BLK, points), orbitals.dtype),
            pltpu.VMEM((list_len + 1, BLK, points), orbitals.dtype),
            pltpu.VMEM((slots + 1, BLK, all_points), orbitals.dtype),
            pltpu.VMEM((row_cap * BLK, all_points), orbitals.dtype),
            pltpu.VMEM(harmonics.shape, harmonics.dtype),
            pltpu.VMEM((8, all_points), jnp.float32),
            pltpu.VMEM((8, all_points), jnp.float32),
            pltpu.VMEM((8, LANES), jnp.float32),
            pltpu.VMEM((devices, 8, LANES), jnp.float32),
            pltpu.VMEM((2, HALF, dens.shape[1]), jnp.float32),
            dma((steps, HALVES, group)),
            dma((steps, HALVES, group)),
            dma((ring_sems, HALVES, row_blocks)),
            dma((ring_sems, HALVES, row_blocks)),
            dma((HALVES,)),
            dma((group,)),
            dma((group,)),
            dma((2,)),
            dma((4,)),
            dma((4,)),
            dma((devices,)),
            dma((devices,)),
            dma((2,)),
        ],
        compiler_params=pltpu.CompilerParams(
            collective_id=1, has_side_effects=True, vmem_limit_bytes=VMEM_BYTES
        ),
        name="grid_step",
    )(block_slot, region_blocks, lists, counts, weights, dens, orbitals, harmonics)


def per_device(
    region, density, block_slot, region_blocks, basis_lists, point_counts, orbitals, weights, harmonics
):
    wide = lax.axis_size("wide")
    narrow = lax.axis_size("narrow")
    devices = wide * narrow
    steps = math.gcd(wide, RING)
    inner = wide // steps
    row_cap = max(1, region // wide)
    col_cap = region // narrow

    components = harmonics.shape[1]
    batches, _, points = orbitals.shape
    total_points = batches * points * devices
    return whole_step(
        block_slot,
        region_blocks,
        basis_lists,
        point_counts,
        weights,
        density,
        orbitals.reshape(batches, -1, BLK, points),
        harmonics,
        steps,
        inner,
        narrow,
        (row_cap, col_cap),
        math.sqrt(total_points * components),
    )


def solution(mesh):
    devices = mesh.shape["wide"] * mesh.shape["narrow"]

    def whole(density, block_slot, region_blocks, *others):
        region = region_blocks.shape[0] // devices
        in_specs = (
            P("wide", "narrow"),
            P(),
            P(("wide", "narrow")),
            P(("wide", "narrow"), None),
            P(("wide", "narrow")),
            P(("wide", "narrow"), None, None),
            P(("wide", "narrow"), None),
            P(("wide", "narrow"), None, None),
        )
        mapped = jax.shard_map(
            functools.partial(per_device, region),
            mesh=mesh,
            in_specs=in_specs,
            out_specs=P("wide", "narrow"),
            check_vma=False,
        )
        return mapped(density, block_slot, region_blocks, *others)

    return whole
```

```python
import functools
import math

import jax
import jax.numpy as jnp
from jax import lax
from jax.experimental import pallas as pl
from jax.experimental.pallas import tpu as pltpu
from jax.sharding import PartitionSpec as P

BLK = 128
FAR_COEFF = 10.0
RING = 4
LANES = 128
CHUNK = 512
HALVES = 2
HALF = BLK // HALVES
MESH = pl.DeviceIdType.MESH
VMEM_BYTES = 63 * 1024 * 1024


def ring_device(shift, inner):
    wide = lax.axis_size("wide")
    return (lax.rem(lax.axis_index("wide") + shift * inner + wide, wide), lax.axis_index("narrow"))


def any_device(offset):
    narrow = lax.axis_size("narrow")
    devices = lax.axis_size("wide") * narrow
    mine = lax.axis_index("wide") * narrow + lax.axis_index("narrow")
    other = lax.rem(mine + offset, devices)
    return mine, (other // narrow, other % narrow)


def trades(inner, narrow):
    return inner == 2 and narrow == 4 and HALVES == 2


def step_kernel(
    steps,
    inner,
    narrow,
    row_cap,
    col_cap,
    far_scale,
    slot_ref,
    region_ref,
    lists_ref,
    counts_ref,
    weights_ref,
    dens_ref,
    orb_ref,
    harm_ref,
    out_ref,
    *rest,
):
    count = steps * HALVES
    raws = [rest[step * HALVES : (step + 1) * HALVES] for step in range(steps)]
    arrs = [rest[count + step * HALVES : count + (step + 1) * HALVES] for step in range(steps)]
    rest = rest[2 * count :]
    square = trades(inner, narrow)
    if square:
        swaps, swap_send, swap_recv = rest[:HALVES], rest[HALVES], rest[HALVES + 1]
        rest = rest[HALVES + 2 :]
    (
        chosen,
        slot_of,
        region_of,
        lists,
        counts,
        weights,
        places,
        tile,
        own_inv,
        inv,
        tables,
        table,
        even,
        odd,
        phi,
        rows,
        harms,
        rho,
        factor,
        share,
        shares,
        ostage,
        send_sem,
        recv_sem,
        ring_send,
        ring_recv,
        load_sem,
        tile_send,
        tile_recv,
        orb_sem,
        local_sem,
        int_sem,
        share_send,
        share_recv,
        out_sem,
    ) = rest
    devices = lax.axis_size("wide") * narrow
    group = inner * narrow
    cap = row_cap * col_cap
    wide_me = lax.axis_index("wide")
    inner_me = wide_me % inner
    ring_me = wide_me // inner
    base = ring_me * inner
    narrow_me = lax.axis_index("narrow")
    mine = inner_me * narrow + narrow_me
    col_blocks = dens_ref.shape[1] // BLK
    row_blocks = dens_ref.shape[0] // BLK
    held = row_blocks * col_blocks
    empty = group * cap
    batches, list_len, _, points = orb_ref.shape
    all_points = batches * points
    slots = narrow * col_cap
    tall = row_cap * BLK
    broad = col_cap * BLK

    def target(place):
        across = lax.rem(inner_me + place // narrow, inner)
        along = lax.rem(narrow_me + place % narrow, narrow)
        return across, along

    def source(place):
        across = lax.rem(inner_me + inner - place // narrow, inner)
        along = lax.rem(narrow_me + narrow - place % narrow, narrow)
        return across, along

    def load_copy(half, place):
        row, col = place // col_blocks, place % col_blocks
        return pltpu.make_async_copy(
            dens_ref.at[
                pl.ds(pl.multiple_of(row * BLK + half * HALF, HALF), HALF),
                pl.ds(pl.multiple_of(col * BLK, BLK), BLK),
            ],
            raws[0][half].at[place],
            load_sem.at[half],
        )

    def loaded(half):
        pltpu.make_async_copy(raws[0][half], raws[0][half], load_sem.at[half]).wait()

    stages = (even, odd)

    def orb_copy(batch, which):
        return pltpu.make_async_copy(
            orb_ref.at[batch], stages[which].at[pl.ds(0, list_len)], orb_sem.at[which]
        )

    def block_copy(step, half, place):
        across, along = target(place)
        return pltpu.make_async_remote_copy(
            src_ref=chosen.at[step % 2, half, place],
            dst_ref=arrs[step][half].at[pl.ds(mine * cap, cap)],
            send_sem=send_sem.at[step, half, place],
            recv_sem=recv_sem.at[step, half, place],
            device_id=(base + across, along),
            device_id_type=MESH,
        )

    def ring_copy(step, half, piece):
        span = pl.ds(piece * col_blocks, col_blocks)
        return pltpu.make_async_remote_copy(
            src_ref=raws[step][half].at[span],
            dst_ref=raws[step + 1][half].at[span],
            send_sem=ring_send.at[step, half, piece],
            recv_sem=ring_recv.at[step, half, piece],
            device_id=ring_device(1, inner),
            device_id_type=MESH,
        )

    def swap_place(half):
        if half == 0:
            return 1 - inner_me, narrow_me
        return inner_me, lax.rem(narrow_me + narrow // 2, narrow)

    def swap_copy(half):
        across, along = swap_place(half)
        return pltpu.make_async_remote_copy(
            src_ref=raws[0][half],
            dst_ref=swaps[half],
            send_sem=swap_send.at[half],
            recv_sem=swap_recv.at[half],
            device_id=(base + across, along),
            device_id_type=MESH,
        )

    def over_blocks(step, half, act, first=1, last=group, plain=False):
        local = (narrow, narrow // 2)[half] if square and step == 0 and not plain else 0

        def body(place, carry):
            if local:

                @pl.when(place != local)
                def _():
                    act(block_copy(step, half, place))

            else:
                act(block_copy(step, half, place))
            return carry

        lax.fori_loop(first, last, body, 0)

    def tile_copy(place):
        across, along = target(place)
        return pltpu.make_async_remote_copy(
            src_ref=tile,
            dst_ref=tables.at[mine],
            send_sem=tile_send.at[place],
            recv_sem=tile_recv.at[place],
            device_id=(base + across, along),
            device_id_type=MESH,
        )

    def share_copy(offset):
        whose, device = any_device(offset)
        return pltpu.make_async_remote_copy(
            src_ref=share,
            dst_ref=shares.at[whose],
            send_sem=share_send.at[offset],
            recv_sem=share_recv.at[offset],
            device_id=device,
            device_id_type=MESH,
        )

    def over(first, last, make, act):
        def body(index, carry):
            act(make(index))
            return carry

        lax.fori_loop(first, last, body, 0)

    start = lambda copy: copy.start()
    wait = lambda copy: copy.wait()
    wait_send = lambda copy: copy.wait_send()
    wait_recv = lambda copy: copy.wait_recv()

    barrier = pltpu.get_barrier_semaphore()

    def greet(place, carry):
        across, along = target(place)
        pl.semaphore_signal(barrier, inc=1, device_id=(base + across, along), device_id_type=MESH)
        return carry

    lax.fori_loop(1, group, greet, 0)
    if steps > 1:
        for shift in (1, -1):
            pl.semaphore_signal(
                barrier, inc=1, device_id=ring_device(shift, inner), device_id_type=MESH
            )
    integers = [
        pltpu.make_async_copy(given, held_in, int_sem.at[index])
        for index, (given, held_in) in enumerate(
            ((slot_ref, slot_of), (region_ref, region_of), (lists_ref, lists), (counts_ref, counts))
        )
    ]
    for copy in integers:
        copy.start()
    for half in range(HALVES):
        over(0, held, functools.partial(load_copy, half), start)
    for which in range(min(2, batches)):
        orb_copy(which, which).start()
    load_harms = pltpu.make_async_copy(harm_ref, harms, local_sem.at[0])
    load_harms.start()
    load_weights = pltpu.make_async_copy(weights_ref, weights, local_sem.at[2])
    load_weights.start()
    for step in range(steps):
        for half in range(HALVES):
            arrs[step][half][empty] = jnp.zeros((HALF, BLK), chosen.dtype)
    for stage in stages:
        stage[list_len] = jnp.zeros((BLK, points), stage.dtype)
    phi[slots] = jnp.zeros((BLK, all_points), phi.dtype)
    rho[...] = jnp.zeros_like(rho)
    for copy in integers:
        copy.wait()

    region = region_of.shape[0]
    wide = lax.axis_size("wide")
    named = [slot_of[region_of[spot]] for spot in range(region)]
    lane = lax.broadcasted_iota(jnp.int32, (8, LANES), 1)
    line = lax.broadcasted_iota(jnp.int32, (8, LANES), 0)
    far = 1 << 20
    row_table = jnp.zeros((8, LANES), jnp.int32)
    col_table = jnp.zeros((8, LANES), jnp.int32)
    row_back = jnp.full((8, LANES), far, jnp.int32)
    col_back = jnp.full((8, LANES), far, jnp.int32)
    cross = jnp.full((8, LANES), slots, jnp.int32)
    row_owners = [lax.rem(slot, wide) for slot in named]
    col_owners = [lax.rem(slot, narrow) for slot in named]
    for spot in range(region):
        row_local, col_local = named[spot] // wide, named[spot] // narrow
        row_rank, col_rank = jnp.int32(0), jnp.int32(0)
        for earlier in range(spot):
            row_rank += (row_owners[earlier] == row_owners[spot]).astype(jnp.int32)
            col_rank += (col_owners[earlier] == col_owners[spot]).astype(jnp.int32)
        row_place = row_owners[spot] * row_cap + row_rank
        col_place = col_owners[spot] * col_cap + col_rank
        places[spot] = col_place
        row_table = jnp.where(lane == row_place, row_local, row_table)
        col_table = jnp.where(lane == col_place, col_local, col_table)
        row_back = jnp.where(
            lane == row_owners[spot] * row_blocks + row_local, row_rank * col_cap, row_back
        )
        col_back = jnp.where(lane == col_owners[spot] * col_blocks + col_local, col_rank, col_back)
        cross = jnp.where(lane == row_place, col_place, cross)
    index_tile = jnp.where(line == 0, row_table, cross)
    index_tile = jnp.where(line == 1, col_table, index_tile)
    index_tile = jnp.where(line == 2, row_back, index_tile)
    index_tile = jnp.where(line == 3, col_back, index_tile)
    tile[...] = index_tile
    tables[mine] = index_tile
    pl.semaphore_wait(barrier, group - 1 + (2 if steps > 1 else 0))
    over(1, group, tile_copy, start)

    def pass_on(step, half):
        for piece in range(row_blocks):
            if step > 0:
                ring_copy(step - 1, half, piece).wait_recv()
            if step < steps - 1:
                ring_copy(step, half, piece).start()

    def pick(step, half, place, put):
        across, along = target(place)
        other = across * narrow + along
        ring = lax.rem(ring_me - step + steps, steps)
        for rr in range(row_cap):
            row = table[other, 0, (ring * inner + inner_me) * row_cap + rr] * col_blocks
            for cr in range(col_cap):
                spot = row + table[other, 1, narrow_me * col_cap + cr]
                put(rr * col_cap + cr, raws[step][half][spot])

    def send_picks(step, half):
        if step >= 2:
            over_blocks(step - 2, half, wait_send)

        def put_own(index, value):
            arrs[step][half][mine * cap + index] = value

        def body(count, carry):
            place = group - 1 - count

            def put(index, value):
                chosen[step % 2, half, place, index] = value

            pick(step, half, place, put)

            @pl.when(count > 0)
            def _():
                block_copy(step, half, place + 1).start()

            return carry

        lax.fori_loop(0, group - 1, body, 0)
        pick(step, half, 0, put_own)
        block_copy(step, half, 1).start()

    def trade(half, ours):
        other_side = swap_place(half)
        across_s, along_s = (inner_me, narrow_me) if ours else other_side
        held_in = raws[0][half] if ours else swaps[half]
        slot = (across_s * narrow + along_s) * cap

        def choose(across, along, put):
            one = across * narrow + along
            for rr in range(row_cap):
                row = table[one, 0, (base + across_s) * row_cap + rr] * col_blocks
                for cr in range(col_cap):
                    spot = row + table[one, 1, along_s * col_cap + cr]
                    put(rr * col_cap + cr, held_in[spot])

        def put_own(index, value):
            arrs[0][half][slot + index] = value

        copies = []
        for turn in (1, 2, 3):
            if half == 0:
                across, along = inner_me, lax.rem(narrow_me + turn, narrow)
            else:
                across = lax.rem(inner_me + turn // 2, inner)
                along = narrow_me // 2 * 2 + lax.rem(narrow_me + turn, 2)
            place = lax.rem(across + inner - across_s, inner) * narrow + lax.rem(
                along + narrow - along_s, narrow
            )

            def put(index, value, place=place):
                chosen[0, half, place, index] = value

            choose(across, along, put)
            copies.append(
                pltpu.make_async_remote_copy(
                    src_ref=chosen.at[0, half, place],
                    dst_ref=arrs[0][half].at[pl.ds(slot, cap)],
                    send_sem=send_sem.at[0, half, place],
                    recv_sem=recv_sem.at[0, half, place],
                    device_id=(base + across, along),
                    device_id_type=MESH,
                )
            )
            if len(copies) > 1:
                copies[-2].start()
        choose(inner_me, narrow_me, put_own)
        copies[-1].start()

    def density_piece(step, halves, place):
        across, along = source(place)
        first = (across * narrow + along) * cap
        ring = lax.rem(ring_me - step + steps, steps)
        owner = (ring * inner + across) * row_cap
        block = jnp.concatenate(
            [
                jnp.concatenate(
                    [arrs[step][half][first + rr * col_cap + cr] for cr in range(col_cap)], axis=1
                )
                for rr in range(row_cap)
                for half in halves
            ],
            axis=0,
        )
        spots = [table[mine, 4, owner + rr] for rr in range(row_cap)]
        down = pl.ds(along * col_cap, col_cap)
        low, size = halves[0] * HALF, len(halves) * HALF

        def chunk(index, carry):
            span = pl.ds(pl.multiple_of(index * CHUNK, CHUNK), CHUNK)
            wave = phi[down, :, span].reshape(broad, CHUNK)
            product = jnp.dot(block, wave, preferred_element_type=jnp.float32)
            total = rho[:, span]
            for rr in range(row_cap):
                mate = phi[spots[rr], low : low + size, span]
                part = product[rr * size : (rr + 1) * size] * mate.astype(jnp.float32)
                total += jnp.sum(part.reshape(size // 8, 8, CHUNK), axis=0)
            rho[:, span] = total
            return carry

        lax.fori_loop(0, all_points // CHUNK, chunk, 0, unroll=True)

    def density_pieces(step, halves, first, last):
        def body(count, carry):
            place = group - 1 - count
            for half in halves:
                over_blocks(step, half, wait_recv, place, place + 1)
            density_piece(step, halves, place)
            return carry

        lax.fori_loop(first, last, body, 0)

    def build(batch, which):
        orb_copy(batch, which).wait()
        across = pl.ds(pl.multiple_of(batch * points, points), points)
        for slot in range(slots):
            phi[slot, :, across] = stages[which][inv[batch, slot]]

        @pl.when(batch + 2 < batches)
        def _():
            orb_copy(batch + 2, which).start()

    def build_pair(pair, carry):
        for which in range(2):
            build(pair * 2 + which, which)
        return carry

    both = tuple(range(HALVES))
    for half in both:
        loaded(half)
        if square:
            swap_copy(half).start()
        pass_on(0, half)
    over(1, group, tile_copy, wait)
    to_table = pltpu.make_async_copy(tables, table, local_sem.at[1])
    to_table.start()
    to_table.wait()
    for half in both:
        if square:
            trade(half, True)
        else:
            send_picks(0, half)
    for batch in range(batches):
        found = jnp.full((8, LANES), list_len, jnp.int32)
        for spot in range(list_len):
            found = jnp.where(lane == places[lists[spot, batch]], spot, found)
        own_inv[batch : batch + 1, :] = found[0:1]
    to_inv = pltpu.make_async_copy(own_inv, inv, local_sem.at[3])
    to_inv.start()
    to_inv.wait()
    lax.fori_loop(0, batches // 2, build_pair, 0)
    if batches % 2:
        build(batches - 1, 0)
    if square:
        for half in both:
            swap_copy(half).wait_recv()
            trade(half, False)
    for step in range(1, steps):
        middle = group // 2 if step > 1 else 0
        pass_on(step, 0)
        send_picks(step, 0)
        density_pieces(step - 1, both, 0, middle)
        pass_on(step, 1)
        send_picks(step, 1)
        density_pieces(step - 1, both, middle, group - 1)
        density_piece(step - 1, both, 0)
    for half in both:
        density_piece(steps - 1, (half,), 0)
        density_pieces(steps - 1, (half,), 0, group - 1)

    load_harms.wait()
    load_weights.wait()

    def live_row(batch):
        point = lax.broadcasted_iota(jnp.int32, (1, points), 1)
        return jnp.where(
            point < counts[batch], weights[pl.ds(batch, 1), :], jnp.float32(0.0)
        )

    components = harms.shape[1]
    moment = jnp.zeros((components, points), jnp.float32)
    for batch in range(batches):
        across = slice(batch * points, (batch + 1) * points)
        dens = jnp.sum(rho[:, across], axis=0, keepdims=True)
        rho[0:1, across] = dens
        moment += harms[batch].astype(jnp.float32) * (live_row(batch) * dens)
    diagonal = lax.broadcasted_iota(jnp.int32, (components, LANES), 0) == lax.broadcasted_iota(
        jnp.int32, (components, LANES), 1
    )
    summed = jnp.sum(moment, axis=1, keepdims=True)
    line = jnp.sum(jnp.where(diagonal, summed, 0.0), axis=0, keepdims=True)
    share[...] = jnp.broadcast_to(line, share.shape)
    whose, _ = any_device(0)
    shares[whose] = jnp.broadcast_to(line, share.shape)
    for half in both:
        for step in range(steps - 1):
            over(0, row_blocks, functools.partial(ring_copy, step, half), wait_send)
        for step in range(max(0, steps - 2), steps):
            over_blocks(step, half, wait_send)
    if square:
        for half in both:
            swap_copy(half).wait_send()
    over(1, devices, share_copy, start)
    over(1, devices, share_copy, wait)
    line = jnp.sum(shares[...], axis=0)[0:1]
    total_moment = jnp.sum(jnp.where(diagonal, line, 0.0), axis=1, keepdims=True)
    for batch in range(batches):
        across = slice(batch * points, (batch + 1) * points)
        dens = rho[0:1, across]
        far = FAR_COEFF * jnp.sum(
            total_moment * harms[batch].astype(jnp.float32), axis=0, keepdims=True
        )
        sixth = jnp.exp(jnp.log(1.0 + dens * dens) * (1.0 / 6.0))
        potential = 0.5 * dens - sixth + far / far_scale
        factor[:, across] = jnp.broadcast_to(live_row(batch) * potential, (8, points))

    def scale_rows(step, across):
        ring = lax.rem(ring_me - 1 - step + 2 * steps, steps)
        owner = (ring * inner + across) * row_cap
        spots = [table[mine, 4, owner + rr] for rr in range(row_cap)]

        def chunk(index, carry):
            span = pl.ds(pl.multiple_of(index * CHUNK, CHUNK), CHUNK)
            for rr in range(row_cap):
                mate = phi[spots[rr], :, span]
                scaled = mate.astype(jnp.float32) * factor[0:1, span]
                rows[rr * BLK : (rr + 1) * BLK, span] = scaled.astype(rows.dtype)
            return carry

        lax.fori_loop(0, all_points // CHUNK, chunk, 0)

    def integral_piece(along, put):
        down = pl.ds(along * col_cap, col_cap)
        term = lax.dot_general(
            rows[...],
            phi[down].reshape(broad, all_points),
            (((1,), (1,)), ((), ())),
            preferred_element_type=jnp.float32,
        )
        for rr in range(row_cap):
            for cr in range(col_cap):
                value = term[rr * BLK : (rr + 1) * BLK, cr * BLK : (cr + 1) * BLK]
                put(rr * col_cap + cr, value.astype(chosen.dtype))

    def send_integrals(step):
        if step >= 2:
            for half in both:
                over_blocks(step - 2, half, wait_send, plain=True)

        def piece(place):
            _, along = target(place)

            def put(index, value):
                for half in both:
                    chosen[step % 2, half, place, index] = value[half * HALF : (half + 1) * HALF]

            integral_piece(along, put)

            @pl.when(place < group - 1)
            def _():
                block_copy(step, 0, place + 1).start()

        def far_rows(count, carry):
            shift = inner - 1 - count
            scale_rows(step, lax.rem(inner_me + shift, inner))

            def body(index, inner_carry):
                piece(shift * narrow + narrow - 1 - index)
                return inner_carry

            lax.fori_loop(0, narrow, body, 0)
            return carry

        lax.fori_loop(0, inner - 1, far_rows, 0)
        scale_rows(step, inner_me)

        def near(index, carry):
            piece(narrow - 1 - index)
            return carry

        lax.fori_loop(0, narrow - 1, near, 0)

        def put_own(index, value):
            for half in both:
                arrs[step][half][mine * cap + index] = value[half * HALF : (half + 1) * HALF]

        integral_piece(narrow_me, put_own)
        block_copy(step, 0, 1).start()

        def later(count, carry):
            block_copy(step, 1, group - 1 - count).start()
            return carry

        lax.fori_loop(0, group - 1, later, 0)

    def out_copy(half, piece):
        first = pl.multiple_of(piece * BLK + half * HALF, HALF)
        return pltpu.make_async_copy(
            ostage.at[piece % 2], out_ref.at[pl.ds(first, HALF)], out_sem.at[piece % 2]
        )

    def add_up(step, half):
        last = step == steps - 1
        ring = lax.rem(ring_me - 1 - step + 2 * steps, steps)
        over(1, group, functools.partial(block_copy, step, half), wait_recv)
        for piece in range(row_blocks):
            if step > 0:
                ring_copy(step - 1, half, piece).wait_recv()
            if last and piece >= 2:
                out_copy(half, piece - 2).wait()
            bases = [
                table[one, 2, (ring * inner + inner_me) * row_blocks + piece] + one * cap
                for one in range(group)
            ]

            def add_block(block, carry, piece=piece, bases=bases):
                spot = piece * col_blocks + block
                if step > 0:
                    total = raws[step][half][spot].astype(jnp.float32)
                else:
                    total = jnp.zeros((HALF, BLK), jnp.float32)
                for one in range(group):
                    col = table[one, 3, narrow_me * col_blocks + block]
                    place = jnp.minimum(bases[one] + col, empty)
                    total += arrs[step][half][place].astype(jnp.float32)
                if last:
                    across = pl.ds(pl.multiple_of(block * BLK, BLK), BLK)
                    ostage[piece % 2, :, across] = total
                else:
                    raws[step][half][spot] = total.astype(chosen.dtype)
                return carry

            lax.fori_loop(0, col_blocks, add_block, 0)
            if last:
                out_copy(half, piece).start()
            elif piece > 0:
                ring_copy(step, half, piece - 1).start()
        if not last:
            ring_copy(step, half, row_blocks - 1).start()
        else:
            for piece in range(max(0, row_blocks - 2), row_blocks):
                out_copy(half, piece).wait()

    send_integrals(0)
    for step in range(steps):
        add_up(step, 0)
        if step + 1 < steps:
            send_integrals(step + 1)
        add_up(step, 1)
    for half in both:
        for step in range(max(0, steps - 2), steps):
            over(1, group, functools.partial(block_copy, step, half), wait_send)
        for step in range(steps - 1):
            over(0, row_blocks, functools.partial(ring_copy, step, half), wait_send)


def whole_step(
    block_slot, region_blocks, lists, counts, weights, dens, orbitals, harmonics, steps, inner, narrow, caps, far_scale
):
    row_cap, col_cap = caps
    group = inner * narrow
    cap = row_cap * col_cap
    devices = steps * group
    ring_sems = max(1, steps - 1)
    row_blocks, col_blocks = dens.shape[0] // BLK, dens.shape[1] // BLK
    held = row_blocks * col_blocks
    batches, list_len, _, points = orbitals.shape
    all_points = batches * points
    components = harmonics.shape[1]
    slots = narrow * col_cap
    ints = jnp.int32
    anywhere = pl.BlockSpec(memory_space=pl.ANY)
    dma = pltpu.SemaphoreType.DMA
    swap_scratch = []
    if trades(inner, narrow):
        swap_scratch = [pltpu.VMEM((held, HALF, BLK), dens.dtype)] * HALVES
        swap_scratch += [dma((HALVES,)), dma((HALVES,))]
    return pl.pallas_call(
        functools.partial(step_kernel, steps, inner, narrow, row_cap, col_cap, far_scale),
        out_shape=jax.ShapeDtypeStruct(dens.shape, jnp.float32),
        in_specs=[anywhere] * 8,
        out_specs=anywhere,
        scratch_shapes=[pltpu.VMEM((held, HALF, BLK), dens.dtype)] * (steps * HALVES)
        + [pltpu.VMEM((group * cap + 1, HALF, BLK), dens.dtype)] * (steps * HALVES)
        + swap_scratch
        + [
            pltpu.VMEM((2, HALVES, group, cap, HALF, BLK), dens.dtype),
            pltpu.SMEM(block_slot.shape, ints),
            pltpu.SMEM(region_blocks.shape, ints),
            pltpu.SMEM(lists.shape, ints),
            pltpu.SMEM(counts.shape, ints),
            pltpu.VMEM(weights.shape, weights.dtype),
            pltpu.SMEM(region_blocks.shape, ints),
            pltpu.VMEM((8, LANES), ints),
            pltpu.VMEM((-(-batches // 8) * 8, LANES), ints),
            pltpu.SMEM((-(-batches // 8) * 8, LANES), ints),
            pltpu.VMEM((group, 8, LANES), ints),
            pltpu.SMEM((group, 8, LANES), ints),
            pltpu.VMEM((list_len + 1, BLK, points), orbitals.dtype),
            pltpu.VMEM((list_len + 1, BLK, points), orbitals.dtype),
            pltpu.VMEM((slots + 1, BLK, all_points), orbitals.dtype),
            pltpu.VMEM((row_cap * BLK, all_points), orbitals.dtype),
            pltpu.VMEM(harmonics.shape, harmonics.dtype),
            pltpu.VMEM((8, all_points), jnp.float32),
            pltpu.VMEM((8, all_points), jnp.float32),
            pltpu.VMEM((8, LANES), jnp.float32),
            pltpu.VMEM((devices, 8, LANES), jnp.float32),
            pltpu.VMEM((2, HALF, dens.shape[1]), jnp.float32),
            dma((steps, HALVES, group)),
            dma((steps, HALVES, group)),
            dma((ring_sems, HALVES, row_blocks)),
            dma((ring_sems, HALVES, row_blocks)),
            dma((HALVES,)),
            dma((group,)),
            dma((group,)),
            dma((2,)),
            dma((4,)),
            dma((4,)),
            dma((devices,)),
            dma((devices,)),
            dma((2,)),
        ],
        compiler_params=pltpu.CompilerParams(
            collective_id=1, has_side_effects=True, vmem_limit_bytes=VMEM_BYTES
        ),
        name="grid_step",
    )(block_slot, region_blocks, lists, counts, weights, dens, orbitals, harmonics)


def per_device(
    region, density, block_slot, region_blocks, basis_lists, point_counts, orbitals, weights, harmonics
):
    wide = lax.axis_size("wide")
    narrow = lax.axis_size("narrow")
    devices = wide * narrow
    steps = math.gcd(wide, RING)
    inner = wide // steps
    row_cap = max(1, region // wide)
    col_cap = region // narrow

    components = harmonics.shape[1]
    batches, _, points = orbitals.shape
    total_points = batches * points * devices
    return whole_step(
        block_slot,
        region_blocks,
        basis_lists.T,
        point_counts,
        weights,
        density,
        orbitals.reshape(batches, -1, BLK, points),
        harmonics,
        steps,
        inner,
        narrow,
        (row_cap, col_cap),
        math.sqrt(total_points * components),
    )


def solution(mesh):
    devices = mesh.shape["wide"] * mesh.shape["narrow"]

    def whole(density, block_slot, region_blocks, *others):
        region = region_blocks.shape[0] // devices
        in_specs = (
            P("wide", "narrow"),
            P(),
            P(("wide", "narrow")),
            P(("wide", "narrow"), None),
            P(("wide", "narrow")),
            P(("wide", "narrow"), None, None),
            P(("wide", "narrow"), None),
            P(("wide", "narrow"), None, None),
        )
        mapped = jax.shard_map(
            functools.partial(per_device, region),
            mesh=mesh,
            in_specs=in_specs,
            out_specs=P("wide", "narrow"),
            check_vma=False,
        )
        return mapped(density, block_slot, region_blocks, *others)

    return whole
```

```python
import functools
import math

import jax
import jax.numpy as jnp
from jax import lax
from jax.experimental import pallas as pl
from jax.experimental.pallas import tpu as pltpu
from jax.sharding import PartitionSpec as P

BLK = 128
FAR_COEFF = 10.0
RING = 4
LANES = 128
CHUNK = 512
HALVES = 2
HALF = BLK // HALVES
MESH = pl.DeviceIdType.MESH
VMEM_BYTES = 63 * 1024 * 1024


def ring_device(shift, inner):
    wide = lax.axis_size("wide")
    return (lax.rem(lax.axis_index("wide") + shift * inner + wide, wide), lax.axis_index("narrow"))


def any_device(offset):
    narrow = lax.axis_size("narrow")
    devices = lax.axis_size("wide") * narrow
    mine = lax.axis_index("wide") * narrow + lax.axis_index("narrow")
    other = lax.rem(mine + offset, devices)
    return mine, (other // narrow, other % narrow)


def trades(inner, narrow):
    return inner == 2 and narrow == 4 and HALVES == 2


def step_kernel(
    steps,
    inner,
    narrow,
    row_cap,
    col_cap,
    far_scale,
    slot_ref,
    region_ref,
    lists_ref,
    counts_ref,
    weights_ref,
    dens_ref,
    orb_ref,
    harm_ref,
    out_ref,
    *rest,
):
    count = steps * HALVES
    raws = [rest[step * HALVES : (step + 1) * HALVES] for step in range(steps)]
    arrs = [rest[count + step * HALVES : count + (step + 1) * HALVES] for step in range(steps)]
    rest = rest[2 * count :]
    square = trades(inner, narrow)
    if square:
        swaps, swap_send, swap_recv = rest[:HALVES], rest[HALVES], rest[HALVES + 1]
        rest = rest[HALVES + 2 :]
    (
        chosen,
        slot_of,
        region_of,
        lists,
        counts,
        weights,
        places,
        tile,
        own_inv,
        inv,
        tables,
        table,
        even,
        odd,
        phi,
        rows,
        harms,
        rho,
        factor,
        share,
        shares,
        ostage,
        send_sem,
        recv_sem,
        ring_send,
        ring_recv,
        load_sem,
        tile_send,
        tile_recv,
        orb_sem,
        local_sem,
        int_sem,
        share_send,
        share_recv,
        out_sem,
    ) = rest
    devices = lax.axis_size("wide") * narrow
    group = inner * narrow
    cap = row_cap * col_cap
    wide_me = lax.axis_index("wide")
    inner_me = wide_me % inner
    ring_me = wide_me // inner
    base = ring_me * inner
    narrow_me = lax.axis_index("narrow")
    mine = inner_me * narrow + narrow_me
    col_blocks = dens_ref.shape[1] // BLK
    row_blocks = dens_ref.shape[0] // BLK
    held = row_blocks * col_blocks
    empty = group * cap
    batches, list_len, _, points = orb_ref.shape
    all_points = batches * points
    slots = narrow * col_cap
    tall = row_cap * BLK
    broad = col_cap * BLK

    def target(place):
        across = lax.rem(inner_me + place // narrow, inner)
        along = lax.rem(narrow_me + place % narrow, narrow)
        return across, along

    def source(place):
        across = lax.rem(inner_me + inner - place // narrow, inner)
        along = lax.rem(narrow_me + narrow - place % narrow, narrow)
        return across, along

    def load_copy(half, place):
        row, col = place // col_blocks, place % col_blocks
        return pltpu.make_async_copy(
            dens_ref.at[
                pl.ds(pl.multiple_of(row * BLK + half * HALF, HALF), HALF),
                pl.ds(pl.multiple_of(col * BLK, BLK), BLK),
            ],
            raws[0][half].at[place],
            load_sem.at[half],
        )

    def loaded(half):
        pltpu.make_async_copy(raws[0][half], raws[0][half], load_sem.at[half]).wait()

    stages = (even, odd)

    def orb_copy(batch, which):
        return pltpu.make_async_copy(
            orb_ref.at[batch], stages[which].at[pl.ds(0, list_len)], orb_sem.at[which]
        )

    def block_copy(step, half, place):
        across, along = target(place)
        return pltpu.make_async_remote_copy(
            src_ref=chosen.at[step % 2, half, place],
            dst_ref=arrs[step][half].at[pl.ds(mine * cap, cap)],
            send_sem=send_sem.at[step, half, place],
            recv_sem=recv_sem.at[step, half, place],
            device_id=(base + across, along),
            device_id_type=MESH,
        )

    def ring_copy(step, half, piece):
        span = pl.ds(piece * col_blocks, col_blocks)
        return pltpu.make_async_remote_copy(
            src_ref=raws[step][half].at[span],
            dst_ref=raws[step + 1][half].at[span],
            send_sem=ring_send.at[step, half, piece],
            recv_sem=ring_recv.at[step, half, piece],
            device_id=ring_device(1, inner),
            device_id_type=MESH,
        )

    def swap_place(half):
        if half == 0:
            return 1 - inner_me, narrow_me
        return inner_me, lax.rem(narrow_me + narrow // 2, narrow)

    def swap_copy(half):
        across, along = swap_place(half)
        return pltpu.make_async_remote_copy(
            src_ref=raws[0][half],
            dst_ref=swaps[half],
            send_sem=swap_send.at[half],
            recv_sem=swap_recv.at[half],
            device_id=(base + across, along),
            device_id_type=MESH,
        )

    def over_blocks(step, half, act, first=1, last=group, plain=False):
        local = (narrow, narrow // 2)[half] if square and step == 0 and not plain else 0

        def body(place, carry):
            if local:

                @pl.when(place != local)
                def _():
                    act(block_copy(step, half, place))

            else:
                act(block_copy(step, half, place))
            return carry

        lax.fori_loop(first, last, body, 0)

    def tile_copy(place):
        across, along = target(place)
        return pltpu.make_async_remote_copy(
            src_ref=tile,
            dst_ref=tables.at[mine],
            send_sem=tile_send.at[place],
            recv_sem=tile_recv.at[place],
            device_id=(base + across, along),
            device_id_type=MESH,
        )

    def share_copy(offset):
        whose, device = any_device(offset)
        return pltpu.make_async_remote_copy(
            src_ref=share,
            dst_ref=shares.at[whose],
            send_sem=share_send.at[offset],
            recv_sem=share_recv.at[offset],
            device_id=device,
            device_id_type=MESH,
        )

    def over(first, last, make, act):
        def body(index, carry):
            act(make(index))
            return carry

        lax.fori_loop(first, last, body, 0)

    start = lambda copy: copy.start()
    wait = lambda copy: copy.wait()
    wait_send = lambda copy: copy.wait_send()
    wait_recv = lambda copy: copy.wait_recv()

    barrier = pltpu.get_barrier_semaphore()

    def greet(place, carry):
        across, along = target(place)
        pl.semaphore_signal(barrier, inc=1, device_id=(base + across, along), device_id_type=MESH)
        return carry

    lax.fori_loop(1, group, greet, 0)
    if steps > 1:
        for shift in (1, -1):
            pl.semaphore_signal(
                barrier, inc=1, device_id=ring_device(shift, inner), device_id_type=MESH
            )
    integers = [
        pltpu.make_async_copy(given, held_in, int_sem.at[index])
        for index, (given, held_in) in enumerate(
            ((slot_ref, slot_of), (region_ref, region_of), (lists_ref, lists), (counts_ref, counts))
        )
    ]
    for copy in integers:
        copy.start()
    for half in range(HALVES):
        over(0, held, functools.partial(load_copy, half), start)
    for which in range(min(2, batches)):
        orb_copy(which, which).start()
    load_harms = pltpu.make_async_copy(harm_ref, harms, local_sem.at[0])
    load_harms.start()
    load_weights = pltpu.make_async_copy(weights_ref, weights, local_sem.at[2])
    load_weights.start()
    for step in range(steps):
        for half in range(HALVES):
            arrs[step][half][empty] = jnp.zeros((HALF, BLK), chosen.dtype)
    for stage in stages:
        stage[list_len] = jnp.zeros((BLK, points), stage.dtype)
    phi[slots] = jnp.zeros((BLK, all_points), phi.dtype)
    rho[...] = jnp.zeros_like(rho)
    for copy in integers:
        copy.wait()

    region = region_of.shape[0]
    wide = lax.axis_size("wide")
    named = [slot_of[region_of[spot]] for spot in range(region)]
    lane = lax.broadcasted_iota(jnp.int32, (8, LANES), 1)
    line = lax.broadcasted_iota(jnp.int32, (8, LANES), 0)
    far = 1 << 20
    row_table = jnp.zeros((8, LANES), jnp.int32)
    col_table = jnp.zeros((8, LANES), jnp.int32)
    row_back = jnp.full((8, LANES), far, jnp.int32)
    col_back = jnp.full((8, LANES), far, jnp.int32)
    cross = jnp.full((8, LANES), slots, jnp.int32)
    row_owners = [lax.rem(slot, wide) for slot in named]
    col_owners = [lax.rem(slot, narrow) for slot in named]
    for spot in range(region):
        row_local, col_local = named[spot] // wide, named[spot] // narrow
        row_rank, col_rank = jnp.int32(0), jnp.int32(0)
        for earlier in range(spot):
            row_rank += (row_owners[earlier] == row_owners[spot]).astype(jnp.int32)
            col_rank += (col_owners[earlier] == col_owners[spot]).astype(jnp.int32)
        row_place = row_owners[spot] * row_cap + row_rank
        col_place = col_owners[spot] * col_cap + col_rank
        places[spot] = col_place
        row_table = jnp.where(lane == row_place, row_local, row_table)
        col_table = jnp.where(lane == col_place, col_local, col_table)
        row_back = jnp.where(
            lane == row_owners[spot] * row_blocks + row_local, row_rank * col_cap, row_back
        )
        col_back = jnp.where(lane == col_owners[spot] * col_blocks + col_local, col_rank, col_back)
        cross = jnp.where(lane == row_place, col_place, cross)
    index_tile = jnp.where(line == 0, row_table, cross)
    index_tile = jnp.where(line == 1, col_table, index_tile)
    index_tile = jnp.where(line == 2, row_back, index_tile)
    index_tile = jnp.where(line == 3, col_back, index_tile)
    tile[...] = index_tile
    tables[mine] = index_tile
    pl.semaphore_wait(barrier, group - 1 + (2 if steps > 1 else 0))
    over(1, group, tile_copy, start)

    def pass_on(step, half):
        for piece in range(row_blocks):
            if step > 0:
                ring_copy(step - 1, half, piece).wait_recv()
            if step < steps - 1:
                ring_copy(step, half, piece).start()

    def pick(step, half, place, put):
        across, along = target(place)
        other = across * narrow + along
        ring = lax.rem(ring_me - step + steps, steps)
        for rr in range(row_cap):
            row = table[other, 0, (ring * inner + inner_me) * row_cap + rr] * col_blocks
            for cr in range(col_cap):
                spot = row + table[other, 1, narrow_me * col_cap + cr]
                put(rr * col_cap + cr, raws[step][half][spot])

    def send_picks(step, half):
        if step >= 2:
            over_blocks(step - 2, half, wait_send)

        def put_own(index, value):
            arrs[step][half][mine * cap + index] = value

        def body(count, carry):
            place = group - 1 - count

            def put(index, value):
                chosen[step % 2, half, place, index] = value

            pick(step, half, place, put)

            @pl.when(count > 0)
            def _():
                block_copy(step, half, place + 1).start()

            return carry

        lax.fori_loop(0, group - 1, body, 0)
        pick(step, half, 0, put_own)
        block_copy(step, half, 1).start()

    def trade(half, ours):
        other_side = swap_place(half)
        across_s, along_s = (inner_me, narrow_me) if ours else other_side
        held_in = raws[0][half] if ours else swaps[half]
        slot = (across_s * narrow + along_s) * cap

        def choose(across, along, put):
            one = across * narrow + along
            for rr in range(row_cap):
                row = table[one, 0, (base + across_s) * row_cap + rr] * col_blocks
                for cr in range(col_cap):
                    spot = row + table[one, 1, along_s * col_cap + cr]
                    put(rr * col_cap + cr, held_in[spot])

        def put_own(index, value):
            arrs[0][half][slot + index] = value

        copies = []
        for turn in (1, 2, 3):
            if half == 0:
                across, along = inner_me, lax.rem(narrow_me + turn, narrow)
            else:
                across = lax.rem(inner_me + turn // 2, inner)
                along = narrow_me // 2 * 2 + lax.rem(narrow_me + turn, 2)
            place = lax.rem(across + inner - across_s, inner) * narrow + lax.rem(
                along + narrow - along_s, narrow
            )

            def put(index, value, place=place):
                chosen[0, half, place, index] = value

            choose(across, along, put)
            copies.append(
                pltpu.make_async_remote_copy(
                    src_ref=chosen.at[0, half, place],
                    dst_ref=arrs[0][half].at[pl.ds(slot, cap)],
                    send_sem=send_sem.at[0, half, place],
                    recv_sem=recv_sem.at[0, half, place],
                    device_id=(base + across, along),
                    device_id_type=MESH,
                )
            )
            if len(copies) > 1:
                copies[-2].start()
        choose(inner_me, narrow_me, put_own)
        copies[-1].start()

    def density_piece(step, halves, place):
        across, along = source(place)
        first = (across * narrow + along) * cap
        ring = lax.rem(ring_me - step + steps, steps)
        owner = (ring * inner + across) * row_cap
        block = jnp.concatenate(
            [
                jnp.concatenate(
                    [arrs[step][half][first + rr * col_cap + cr] for cr in range(col_cap)], axis=1
                )
                for rr in range(row_cap)
                for half in halves
            ],
            axis=0,
        )
        spots = [table[mine, 4, owner + rr] for rr in range(row_cap)]
        down = pl.ds(along * col_cap, col_cap)
        low, size = halves[0] * HALF, len(halves) * HALF

        def chunk(index, carry):
            span = pl.ds(pl.multiple_of(index * CHUNK, CHUNK), CHUNK)
            wave = phi[down, :, span].reshape(broad, CHUNK)
            product = jnp.dot(block, wave, preferred_element_type=jnp.float32)
            total = rho[:, span]
            for rr in range(row_cap):
                mate = phi[spots[rr], low : low + size, span]
                part = product[rr * size : (rr + 1) * size] * mate.astype(jnp.float32)
                total += jnp.sum(part.reshape(size // 8, 8, CHUNK), axis=0)
            rho[:, span] = total
            return carry

        lax.fori_loop(0, all_points // CHUNK, chunk, 0, unroll=True)

    def density_pieces(step, halves, first, last):
        def body(count, carry):
            place = group - 1 - count
            for half in halves:
                over_blocks(step, half, wait_recv, place, place + 1)
            density_piece(step, halves, place)
            return carry

        lax.fori_loop(first, last, body, 0)

    def build(batch, which):
        orb_copy(batch, which).wait()
        across = pl.ds(pl.multiple_of(batch * points, points), points)
        for slot in range(slots):
            phi[slot, :, across] = stages[which][inv[batch, slot]]

        @pl.when(batch + 2 < batches)
        def _():
            orb_copy(batch + 2, which).start()

    def build_pair(pair, carry):
        for which in range(2):
            build(pair * 2 + which, which)
        return carry

    both = tuple(range(HALVES))
    for half in both:
        loaded(half)
        if square:
            swap_copy(half).start()
        pass_on(0, half)
    over(1, group, tile_copy, wait)
    to_table = pltpu.make_async_copy(tables, table, local_sem.at[1])
    to_table.start()
    to_table.wait()
    for half in both:
        if square:
            trade(half, True)
        else:
            send_picks(0, half)
    for batch in range(batches):
        found = jnp.full((8, LANES), list_len, jnp.int32)
        for spot in range(list_len):
            found = jnp.where(lane == places[lists[spot, batch]], spot, found)
        own_inv[batch : batch + 1, :] = found[0:1]
    to_inv = pltpu.make_async_copy(own_inv, inv, local_sem.at[3])
    to_inv.start()
    to_inv.wait()
    lax.fori_loop(0, batches // 2, build_pair, 0)
    if batches % 2:
        build(batches - 1, 0)
    if square:
        for half in both:
            swap_copy(half).wait_recv()
            trade(half, False)
    for step in range(1, steps):
        middle = group // 2 if step > 1 else 0
        pass_on(step, 0)
        send_picks(step, 0)
        density_pieces(step - 1, both, 0, middle)
        pass_on(step, 1)
        send_picks(step, 1)
        density_pieces(step - 1, both, middle, group - 1)
        density_piece(step - 1, both, 0)
    for half in both:
        density_piece(steps - 1, (half,), 0)
        density_pieces(steps - 1, (half,), 0, group - 1)

    load_harms.wait()
    load_weights.wait()

    def live_row(batch):
        point = lax.broadcasted_iota(jnp.int32, (1, points), 1)
        return jnp.where(
            point < counts[batch], weights[pl.ds(batch, 1), :], jnp.float32(0.0)
        )

    components = harms.shape[1]
    moment = jnp.zeros((components, points), jnp.float32)
    for batch in range(batches):
        across = slice(batch * points, (batch + 1) * points)
        dens = jnp.sum(rho[:, across], axis=0, keepdims=True)
        rho[0:1, across] = dens
        moment += harms[batch].astype(jnp.float32) * (live_row(batch) * dens)
    diagonal = lax.broadcasted_iota(jnp.int32, (components, LANES), 0) == lax.broadcasted_iota(
        jnp.int32, (components, LANES), 1
    )
    summed = jnp.sum(moment, axis=1, keepdims=True)
    line = jnp.sum(jnp.where(diagonal, summed, 0.0), axis=0, keepdims=True)
    share[...] = jnp.broadcast_to(line, share.shape)
    whose, _ = any_device(0)
    shares[whose] = jnp.broadcast_to(line, share.shape)
    for half in both:
        for step in range(steps - 1):
            over(0, row_blocks, functools.partial(ring_copy, step, half), wait_send)
        for step in range(max(0, steps - 2), steps):
            over_blocks(step, half, wait_send)
    if square:
        for half in both:
            swap_copy(half).wait_send()
    over(1, devices, share_copy, start)
    over(1, devices, share_copy, wait)
    line = jnp.sum(shares[...], axis=0)[0:1]
    total_moment = jnp.sum(jnp.where(diagonal, line, 0.0), axis=1, keepdims=True)
    for batch in range(batches):
        across = slice(batch * points, (batch + 1) * points)
        dens = rho[0:1, across]
        far = FAR_COEFF * jnp.sum(
            total_moment * harms[batch].astype(jnp.float32), axis=0, keepdims=True
        )
        sixth = jnp.exp(jnp.log(1.0 + dens * dens) * (1.0 / 6.0))
        potential = 0.5 * dens - sixth + far / far_scale
        factor[:, across] = jnp.broadcast_to(live_row(batch) * potential, (8, points))

    def scale_rows(step, across, where):
        ring = lax.rem(ring_me - 1 - step + 2 * steps, steps)
        owner = (ring * inner + across) * row_cap
        spots = [table[mine, 4, owner + rr] for rr in range(row_cap)]

        def chunk(index, carry):
            span = pl.ds(pl.multiple_of(index * CHUNK, CHUNK), CHUNK)
            for rr in range(row_cap):
                mate = phi[spots[rr], :, span]
                scaled = mate.astype(jnp.float32) * factor[0:1, span]
                rows[where, rr * BLK : (rr + 1) * BLK, span] = scaled.astype(rows.dtype)
            return carry

        lax.fori_loop(0, all_points // CHUNK, chunk, 0, unroll=True)

    def integral_piece(along, where, put):
        down = pl.ds(along * col_cap, col_cap)
        term = lax.dot_general(
            rows[where],
            phi[down].reshape(broad, all_points),
            (((1,), (1,)), ((), ())),
            preferred_element_type=jnp.float32,
        )
        for rr in range(row_cap):
            for cr in range(col_cap):
                value = term[rr * BLK : (rr + 1) * BLK, cr * BLK : (cr + 1) * BLK]
                put(rr * col_cap + cr, value.astype(chosen.dtype))

    def send_integrals(step):
        if step >= 2:
            for half in both:
                over_blocks(step - 2, half, wait_send, plain=True)

        def piece(place, where):
            _, along = target(place)

            def put(index, value):
                for half in both:
                    chosen[step % 2, half, place, index] = value[half * HALF : (half + 1) * HALF]

            integral_piece(along, where, put)

        def far_rows(count, carry):
            shift = inner - 1 - count

            @pl.when(count > 0)
            def _():
                scale_rows(step, lax.rem(inner_me + shift, inner), 0)

            def body(index, inner_carry):
                place = shift * narrow + narrow - 1 - index

                @pl.when(place < group - 1)
                def _():
                    piece(place, 0)

                @pl.when(place < group - 2)
                def _():
                    block_copy(step, 0, place + 1).start()

                return inner_carry

            lax.fori_loop(0, narrow, body, 0)
            return carry

        scale_rows(step, lax.rem(inner_me + inner - 1, inner), 0)
        piece(group - 1, 0)
        if inner > 1:
            scale_rows(step, inner_me, 1)
        block_copy(step, 0, group - 1).start()
        lax.fori_loop(0, inner - 1, far_rows, 0)
        home = 1 if inner > 1 else 0

        def near(index, carry):
            place = narrow - 1 - index

            @pl.when(place < group - 1)
            def _():
                piece(place, home)

            @pl.when(place < group - 2)
            def _():
                block_copy(step, 0, place + 1).start()

            return carry

        lax.fori_loop(0, narrow - 1, near, 0)

        def put_own(index, value):
            for half in both:
                arrs[step][half][mine * cap + index] = value[half * HALF : (half + 1) * HALF]

        integral_piece(narrow_me, home, put_own)
        if group > 2:
            block_copy(step, 0, 1).start()

        def later(count, carry):
            block_copy(step, 1, group - 1 - count).start()
            return carry

        lax.fori_loop(0, group - 1, later, 0)

    def out_copy(half, piece):
        first = pl.multiple_of(piece * BLK + half * HALF, HALF)
        return pltpu.make_async_copy(
            ostage.at[piece % 2], out_ref.at[pl.ds(first, HALF)], out_sem.at[piece % 2]
        )

    def add_up(step, half):
        last = step == steps - 1
        ring = lax.rem(ring_me - 1 - step + 2 * steps, steps)
        over(1, group, functools.partial(block_copy, step, half), wait_recv)
        for piece in range(row_blocks):
            if step > 0:
                ring_copy(step - 1, half, piece).wait_recv()
            if last and piece >= 2:
                out_copy(half, piece - 2).wait()
            bases = [
                table[one, 2, (ring * inner + inner_me) * row_blocks + piece] + one * cap
                for one in range(group)
            ]

            def add_block(block, carry, piece=piece, bases=bases):
                spot = piece * col_blocks + block
                if step > 0:
                    total = raws[step][half][spot].astype(jnp.float32)
                else:
                    total = jnp.zeros((HALF, BLK), jnp.float32)
                for one in range(group):
                    col = table[one, 3, narrow_me * col_blocks + block]
                    place = jnp.minimum(bases[one] + col, empty)
                    total += arrs[step][half][place].astype(jnp.float32)
                if last:
                    across = pl.ds(pl.multiple_of(block * BLK, BLK), BLK)
                    ostage[piece % 2, :, across] = total
                else:
                    raws[step][half][spot] = total.astype(chosen.dtype)
                return carry

            lax.fori_loop(0, col_blocks, add_block, 0)
            if last:
                out_copy(half, piece).start()
            elif piece > 0:
                ring_copy(step, half, piece - 1).start()
        if not last:
            ring_copy(step, half, row_blocks - 1).start()
        else:
            for piece in range(max(0, row_blocks - 2), row_blocks):
                out_copy(half, piece).wait()

    send_integrals(0)
    for step in range(steps):
        add_up(step, 0)
        if step + 1 < steps:
            send_integrals(step + 1)
        add_up(step, 1)
    for half in both:
        for step in range(max(0, steps - 2), steps):
            over(1, group, functools.partial(block_copy, step, half), wait_send)
        for step in range(steps - 1):
            over(0, row_blocks, functools.partial(ring_copy, step, half), wait_send)


def whole_step(
    block_slot, region_blocks, lists, counts, weights, dens, orbitals, harmonics, steps, inner, narrow, caps, far_scale
):
    row_cap, col_cap = caps
    group = inner * narrow
    cap = row_cap * col_cap
    devices = steps * group
    ring_sems = max(1, steps - 1)
    row_blocks, col_blocks = dens.shape[0] // BLK, dens.shape[1] // BLK
    held = row_blocks * col_blocks
    batches, list_len, _, points = orbitals.shape
    all_points = batches * points
    components = harmonics.shape[1]
    slots = narrow * col_cap
    ints = jnp.int32
    anywhere = pl.BlockSpec(memory_space=pl.ANY)
    dma = pltpu.SemaphoreType.DMA
    swap_scratch = []
    if trades(inner, narrow):
        swap_scratch = [pltpu.VMEM((held, HALF, BLK), dens.dtype)] * HALVES
        swap_scratch += [dma((HALVES,)), dma((HALVES,))]
    return pl.pallas_call(
        functools.partial(step_kernel, steps, inner, narrow, row_cap, col_cap, far_scale),
        out_shape=jax.ShapeDtypeStruct(dens.shape, jnp.float32),
        in_specs=[anywhere] * 8,
        out_specs=anywhere,
        scratch_shapes=[pltpu.VMEM((held, HALF, BLK), dens.dtype)] * (steps * HALVES)
        + [pltpu.VMEM((group * cap + 1, HALF, BLK), dens.dtype)] * (steps * HALVES)
        + swap_scratch
        + [
            pltpu.VMEM((2, HALVES, group, cap, HALF, BLK), dens.dtype),
            pltpu.SMEM(block_slot.shape, ints),
            pltpu.SMEM(region_blocks.shape, ints),
            pltpu.SMEM(lists.shape, ints),
            pltpu.SMEM(counts.shape, ints),
            pltpu.VMEM(weights.shape, weights.dtype),
            pltpu.SMEM(region_blocks.shape, ints),
            pltpu.VMEM((8, LANES), ints),
            pltpu.VMEM((-(-batches // 8) * 8, LANES), ints),
            pltpu.SMEM((-(-batches // 8) * 8, LANES), ints),
            pltpu.VMEM((group, 8, LANES), ints),
            pltpu.SMEM((group, 8, LANES), ints),
            pltpu.VMEM((list_len + 1, BLK, points), orbitals.dtype),
            pltpu.VMEM((list_len + 1, BLK, points), orbitals.dtype),
            pltpu.VMEM((slots + 1, BLK, all_points), orbitals.dtype),
            pltpu.VMEM((2, row_cap * BLK, all_points), orbitals.dtype),
            pltpu.VMEM(harmonics.shape, harmonics.dtype),
            pltpu.VMEM((8, all_points), jnp.float32),
            pltpu.VMEM((8, all_points), jnp.float32),
            pltpu.VMEM((8, LANES), jnp.float32),
            pltpu.VMEM((devices, 8, LANES), jnp.float32),
            pltpu.VMEM((2, HALF, dens.shape[1]), jnp.float32),
            dma((steps, HALVES, group)),
            dma((steps, HALVES, group)),
            dma((ring_sems, HALVES, row_blocks)),
            dma((ring_sems, HALVES, row_blocks)),
            dma((HALVES,)),
            dma((group,)),
            dma((group,)),
            dma((2,)),
            dma((4,)),
            dma((4,)),
            dma((devices,)),
            dma((devices,)),
            dma((2,)),
        ],
        compiler_params=pltpu.CompilerParams(
            collective_id=1, has_side_effects=True, vmem_limit_bytes=VMEM_BYTES
        ),
        name="grid_step",
    )(block_slot, region_blocks, lists, counts, weights, dens, orbitals, harmonics)


def settle_kernel(given_ref, out_ref, held, sems):
    chunks, size = held.shape[0], held.shape[1]

    def copy(index, out):
        span = pl.ds(index * size, size)
        if out:
            return pltpu.make_async_copy(held.at[index], out_ref.at[span], sems.at[1, index])
        return pltpu.make_async_copy(given_ref.at[span], held.at[index], sems.at[0, index])

    for index in range(chunks):
        copy(index, False).start()
    for index in range(chunks):
        copy(index, False).wait()
        copy(index, True).start()
    for index in range(chunks):
        copy(index, True).wait()


def settle(result):
    chunks = 8
    rows, cols = result.shape
    anywhere = pl.BlockSpec(memory_space=pl.ANY)
    return pl.pallas_call(
        settle_kernel,
        out_shape=jax.ShapeDtypeStruct(result.shape, result.dtype),
        in_specs=[anywhere],
        out_specs=anywhere,
        scratch_shapes=[
            pltpu.VMEM((chunks, rows // chunks, cols), result.dtype),
            pltpu.SemaphoreType.DMA((2, chunks)),
        ],
        compiler_params=pltpu.CompilerParams(vmem_limit_bytes=VMEM_BYTES),
        name="settle",
    )(result)


def per_device(
    region, density, block_slot, region_blocks, basis_lists, point_counts, orbitals, weights, harmonics
):
    wide = lax.axis_size("wide")
    narrow = lax.axis_size("narrow")
    devices = wide * narrow
    steps = math.gcd(wide, RING)
    inner = wide // steps
    row_cap = max(1, region // wide)
    col_cap = region // narrow

    components = harmonics.shape[1]
    batches, _, points = orbitals.shape
    total_points = batches * points * devices
    result = whole_step(
        block_slot,
        region_blocks,
        basis_lists.T,
        point_counts,
        weights,
        density,
        orbitals.reshape(batches, -1, BLK, points),
        harmonics,
        steps,
        inner,
        narrow,
        (row_cap, col_cap),
        math.sqrt(total_points * components),
    )
    return settle(result)


def solution(mesh):
    devices = mesh.shape["wide"] * mesh.shape["narrow"]

    def whole(density, block_slot, region_blocks, *others):
        region = region_blocks.shape[0] // devices
        in_specs = (
            P("wide", "narrow"),
            P(),
            P(("wide", "narrow")),
            P(("wide", "narrow"), None),
            P(("wide", "narrow")),
            P(("wide", "narrow"), None, None),
            P(("wide", "narrow"), None),
            P(("wide", "narrow"), None, None),
        )
        mapped = jax.shard_map(
            functools.partial(per_device, region),
            mesh=mesh,
            in_specs=in_specs,
            out_specs=P("wide", "narrow"),
            check_vma=False,
        )
        return mapped(density, block_slot, region_blocks, *others)

    return whole
```

```python
import functools
import math

import jax
import jax.numpy as jnp
from jax import lax
from jax.experimental import pallas as pl
from jax.experimental.pallas import tpu as pltpu
from jax.sharding import PartitionSpec as P

BLK = 128
FAR_COEFF = 10.0
RING = 4
LANES = 128
CHUNK = 512
HALVES = 2
HALF = BLK // HALVES
MESH = pl.DeviceIdType.MESH
VMEM_BYTES = 63 * 1024 * 1024


def ring_device(shift, inner):
    wide = lax.axis_size("wide")
    return (lax.rem(lax.axis_index("wide") + shift * inner + wide, wide), lax.axis_index("narrow"))


def any_device(offset):
    narrow = lax.axis_size("narrow")
    devices = lax.axis_size("wide") * narrow
    mine = lax.axis_index("wide") * narrow + lax.axis_index("narrow")
    other = lax.rem(mine + offset, devices)
    return mine, (other // narrow, other % narrow)


def trades(inner, narrow):
    return inner == 2 and narrow == 4 and HALVES == 2


def step_kernel(
    steps,
    inner,
    narrow,
    row_cap,
    col_cap,
    far_scale,
    slot_ref,
    region_ref,
    lists_ref,
    counts_ref,
    weights_ref,
    dens_ref,
    orb_ref,
    harm_ref,
    out_ref,
    *rest,
):
    count = steps * HALVES
    raws = [rest[step * HALVES : (step + 1) * HALVES] for step in range(steps)]
    arrs = [rest[count + step * HALVES : count + (step + 1) * HALVES] for step in range(steps)]
    rest = rest[2 * count :]
    square = trades(inner, narrow)
    if square:
        swaps, swap_send, swap_recv = rest[:HALVES], rest[HALVES], rest[HALVES + 1]
        rest = rest[HALVES + 2 :]
    (
        chosen,
        slot_of,
        region_of,
        lists,
        counts,
        weights,
        places,
        tile,
        own_inv,
        inv,
        tables,
        table,
        even,
        odd,
        phi,
        rows,
        harms,
        rho,
        factor,
        share,
        shares,
        ostage,
        send_sem,
        recv_sem,
        ring_send,
        ring_recv,
        load_sem,
        tile_send,
        tile_recv,
        orb_sem,
        local_sem,
        int_sem,
        share_send,
        share_recv,
        out_sem,
    ) = rest
    devices = lax.axis_size("wide") * narrow
    group = inner * narrow
    cap = row_cap * col_cap
    wide_me = lax.axis_index("wide")
    inner_me = wide_me % inner
    ring_me = wide_me // inner
    base = ring_me * inner
    narrow_me = lax.axis_index("narrow")
    mine = inner_me * narrow + narrow_me
    col_blocks = dens_ref.shape[1] // BLK
    row_blocks = dens_ref.shape[0] // BLK
    held = row_blocks * col_blocks
    empty = group * cap
    batches, list_len, _, points = orb_ref.shape
    all_points = batches * points
    slots = narrow * col_cap
    tall = row_cap * BLK
    broad = col_cap * BLK

    def target(place):
        across = lax.rem(inner_me + place // narrow, inner)
        along = lax.rem(narrow_me + place % narrow, narrow)
        return across, along

    def source(place):
        across = lax.rem(inner_me + inner - place // narrow, inner)
        along = lax.rem(narrow_me + narrow - place % narrow, narrow)
        return across, along

    def load_copy(half, place):
        row, col = place // col_blocks, place % col_blocks
        return pltpu.make_async_copy(
            dens_ref.at[
                pl.ds(pl.multiple_of(row * BLK + half * HALF, HALF), HALF),
                pl.ds(pl.multiple_of(col * BLK, BLK), BLK),
            ],
            raws[0][half].at[place],
            load_sem.at[half],
        )

    def loaded(half):
        pltpu.make_async_copy(raws[0][half], raws[0][half], load_sem.at[half]).wait()

    stages = (even, odd)

    def orb_copy(batch, which):
        return pltpu.make_async_copy(
            orb_ref.at[batch], stages[which].at[pl.ds(0, list_len)], orb_sem.at[which]
        )

    def block_copy(step, half, place):
        across, along = target(place)
        return pltpu.make_async_remote_copy(
            src_ref=chosen.at[step % 2, half, place],
            dst_ref=arrs[step][half].at[pl.ds(mine * cap, cap)],
            send_sem=send_sem.at[step, half, place],
            recv_sem=recv_sem.at[step, half, place],
            device_id=(base + across, along),
            device_id_type=MESH,
        )

    def ring_copy(step, half, piece):
        span = pl.ds(piece * col_blocks, col_blocks)
        return pltpu.make_async_remote_copy(
            src_ref=raws[step][half].at[span],
            dst_ref=raws[step + 1][half].at[span],
            send_sem=ring_send.at[step, half, piece],
            recv_sem=ring_recv.at[step, half, piece],
            device_id=ring_device(1, inner),
            device_id_type=MESH,
        )

    def swap_place(half):
        if half == 0:
            return 1 - inner_me, narrow_me
        return inner_me, lax.rem(narrow_me + narrow // 2, narrow)

    def swap_copy(half):
        across, along = swap_place(half)
        return pltpu.make_async_remote_copy(
            src_ref=raws[0][half],
            dst_ref=swaps[half],
            send_sem=swap_send.at[half],
            recv_sem=swap_recv.at[half],
            device_id=(base + across, along),
            device_id_type=MESH,
        )

    def over_blocks(step, half, act, first=1, last=group, plain=False):
        local = (narrow, narrow // 2)[half] if square and step == 0 and not plain else 0

        def body(place, carry):
            if local:

                @pl.when(place != local)
                def _():
                    act(block_copy(step, half, place))

            else:
                act(block_copy(step, half, place))
            return carry

        lax.fori_loop(first, last, body, 0)

    def tile_copy(place):
        across, along = target(place)
        return pltpu.make_async_remote_copy(
            src_ref=tile,
            dst_ref=tables.at[mine],
            send_sem=tile_send.at[place],
            recv_sem=tile_recv.at[place],
            device_id=(base + across, along),
            device_id_type=MESH,
        )

    def share_copy(offset):
        whose, device = any_device(offset)
        return pltpu.make_async_remote_copy(
            src_ref=share,
            dst_ref=shares.at[whose],
            send_sem=share_send.at[offset],
            recv_sem=share_recv.at[offset],
            device_id=device,
            device_id_type=MESH,
        )

    def over(first, last, make, act):
        def body(index, carry):
            act(make(index))
            return carry

        lax.fori_loop(first, last, body, 0)

    start = lambda copy: copy.start()
    wait = lambda copy: copy.wait()
    wait_send = lambda copy: copy.wait_send()
    wait_recv = lambda copy: copy.wait_recv()

    barrier = pltpu.get_barrier_semaphore()

    def greet(place, carry):
        across, along = target(place)
        pl.semaphore_signal(barrier, inc=1, device_id=(base + across, along), device_id_type=MESH)
        return carry

    lax.fori_loop(1, group, greet, 0)
    if steps > 1:
        for shift in (1, -1):
            pl.semaphore_signal(
                barrier, inc=1, device_id=ring_device(shift, inner), device_id_type=MESH
            )
    integers = [
        pltpu.make_async_copy(given, held_in, int_sem.at[index])
        for index, (given, held_in) in enumerate(
            ((slot_ref, slot_of), (region_ref, region_of), (lists_ref, lists), (counts_ref, counts))
        )
    ]
    for copy in integers:
        copy.start()
    for half in range(HALVES):
        over(0, held, functools.partial(load_copy, half), start)
    for which in range(min(2, batches)):
        orb_copy(which, which).start()
    load_harms = pltpu.make_async_copy(harm_ref, harms, local_sem.at[0])
    load_harms.start()
    load_weights = pltpu.make_async_copy(weights_ref, weights, local_sem.at[2])
    load_weights.start()
    for step in range(steps):
        for half in range(HALVES):
            arrs[step][half][empty] = jnp.zeros((HALF, BLK), chosen.dtype)
    for stage in stages:
        stage[list_len] = jnp.zeros((BLK, points), stage.dtype)
    phi[slots] = jnp.zeros((BLK, all_points), phi.dtype)
    rho[...] = jnp.zeros_like(rho)
    for copy in integers:
        copy.wait()

    region = region_of.shape[0]
    wide = lax.axis_size("wide")
    named = [slot_of[region_of[spot]] for spot in range(region)]
    lane = lax.broadcasted_iota(jnp.int32, (8, LANES), 1)
    line = lax.broadcasted_iota(jnp.int32, (8, LANES), 0)
    far = 1 << 20
    row_table = jnp.zeros((8, LANES), jnp.int32)
    col_table = jnp.zeros((8, LANES), jnp.int32)
    row_back = jnp.full((8, LANES), far, jnp.int32)
    col_back = jnp.full((8, LANES), far, jnp.int32)
    cross = jnp.full((8, LANES), slots, jnp.int32)
    row_owners = [lax.rem(slot, wide) for slot in named]
    col_owners = [lax.rem(slot, narrow) for slot in named]
    for spot in range(region):
        row_local, col_local = named[spot] // wide, named[spot] // narrow
        row_rank, col_rank = jnp.int32(0), jnp.int32(0)
        for earlier in range(spot):
            row_rank += (row_owners[earlier] == row_owners[spot]).astype(jnp.int32)
            col_rank += (col_owners[earlier] == col_owners[spot]).astype(jnp.int32)
        row_place = row_owners[spot] * row_cap + row_rank
        col_place = col_owners[spot] * col_cap + col_rank
        places[spot] = col_place
        row_table = jnp.where(lane == row_place, row_local, row_table)
        col_table = jnp.where(lane == col_place, col_local, col_table)
        row_back = jnp.where(
            lane == row_owners[spot] * row_blocks + row_local, row_rank * col_cap, row_back
        )
        col_back = jnp.where(lane == col_owners[spot] * col_blocks + col_local, col_rank, col_back)
        cross = jnp.where(lane == row_place, col_place, cross)
    index_tile = jnp.where(line == 0, row_table, cross)
    index_tile = jnp.where(line == 1, col_table, index_tile)
    index_tile = jnp.where(line == 2, row_back, index_tile)
    index_tile = jnp.where(line == 3, col_back, index_tile)
    tile[...] = index_tile
    tables[mine] = index_tile
    pl.semaphore_wait(barrier, group - 1 + (2 if steps > 1 else 0))
    over(1, group, tile_copy, start)

    def pass_on(step, half):
        for piece in range(row_blocks):
            if step > 0:
                ring_copy(step - 1, half, piece).wait_recv()
            if step < steps - 1:
                ring_copy(step, half, piece).start()

    def sent_on():
        for step in range(steps - 1):
            for half in range(HALVES):
                over(0, row_blocks, functools.partial(ring_copy, step, half), wait_send)

    def pick(step, half, place, put):
        across, along = target(place)
        other = across * narrow + along
        ring = lax.rem(ring_me - step + steps, steps)
        for rr in range(row_cap):
            row = table[other, 0, (ring * inner + inner_me) * row_cap + rr] * col_blocks
            for cr in range(col_cap):
                spot = row + table[other, 1, narrow_me * col_cap + cr]
                put(rr * col_cap + cr, raws[step][half][spot])

    def send_picks(step, half):
        if step >= 2:
            over_blocks(step - 2, half, wait_send)

        def put_own(index, value):
            arrs[step][half][mine * cap + index] = value

        def body(count, carry):
            place = group - 1 - count

            def put(index, value):
                chosen[step % 2, half, place, index] = value

            pick(step, half, place, put)

            @pl.when(count > 0)
            def _():
                block_copy(step, half, place + 1).start()

            return carry

        lax.fori_loop(0, group - 1, body, 0)
        pick(step, half, 0, put_own)
        block_copy(step, half, 1).start()

    def trade(half, ours):
        other_side = swap_place(half)
        across_s, along_s = (inner_me, narrow_me) if ours else other_side
        held_in = raws[0][half] if ours else swaps[half]
        slot = (across_s * narrow + along_s) * cap

        def choose(across, along, put):
            one = across * narrow + along
            for rr in range(row_cap):
                row = table[one, 0, (base + across_s) * row_cap + rr] * col_blocks
                for cr in range(col_cap):
                    spot = row + table[one, 1, along_s * col_cap + cr]
                    put(rr * col_cap + cr, held_in[spot])

        def put_own(index, value):
            arrs[0][half][slot + index] = value

        copies = []
        for turn in (1, 2, 3):
            if half == 0:
                across, along = inner_me, lax.rem(narrow_me + turn, narrow)
            else:
                across = lax.rem(inner_me + turn // 2, inner)
                along = narrow_me // 2 * 2 + lax.rem(narrow_me + turn, 2)
            place = lax.rem(across + inner - across_s, inner) * narrow + lax.rem(
                along + narrow - along_s, narrow
            )

            def put(index, value, place=place):
                chosen[0, half, place, index] = value

            choose(across, along, put)
            copies.append(
                pltpu.make_async_remote_copy(
                    src_ref=chosen.at[0, half, place],
                    dst_ref=arrs[0][half].at[pl.ds(slot, cap)],
                    send_sem=send_sem.at[0, half, place],
                    recv_sem=recv_sem.at[0, half, place],
                    device_id=(base + across, along),
                    device_id_type=MESH,
                )
            )
            if len(copies) > 1:
                copies[-2].start()
        choose(inner_me, narrow_me, put_own)
        copies[-1].start()

    def density_piece(step, halves, place):
        across, along = source(place)
        first = (across * narrow + along) * cap
        ring = lax.rem(ring_me - step + steps, steps)
        owner = (ring * inner + across) * row_cap
        block = jnp.concatenate(
            [
                jnp.concatenate(
                    [arrs[step][half][first + rr * col_cap + cr] for cr in range(col_cap)], axis=1
                )
                for rr in range(row_cap)
                for half in halves
            ],
            axis=0,
        )
        spots = [table[mine, 4, owner + rr] for rr in range(row_cap)]
        down = pl.ds(along * col_cap, col_cap)
        low, size = halves[0] * HALF, len(halves) * HALF

        def chunk(index, carry):
            span = pl.ds(pl.multiple_of(index * CHUNK, CHUNK), CHUNK)
            wave = phi[down, :, span].reshape(broad, CHUNK)
            product = jnp.dot(block, wave, preferred_element_type=jnp.float32)
            total = rho[:, span]
            for rr in range(row_cap):
                mate = phi[spots[rr], low : low + size, span]
                part = product[rr * size : (rr + 1) * size] * mate.astype(jnp.float32)
                total += jnp.sum(part.reshape(size // 8, 8, CHUNK), axis=0)
            rho[:, span] = total
            return carry

        lax.fori_loop(0, all_points // CHUNK, chunk, 0, unroll=True)

    def density_pieces(step, halves, first, last):
        def body(count, carry):
            place = group - 1 - count
            for half in halves:
                over_blocks(step, half, wait_recv, place, place + 1)
            density_piece(step, halves, place)
            return carry

        lax.fori_loop(first, last, body, 0)

    def build(batch, which):
        orb_copy(batch, which).wait()
        across = pl.ds(pl.multiple_of(batch * points, points), points)
        for slot in range(slots):
            phi[slot, :, across] = stages[which][inv[batch, slot]]

        @pl.when(batch + 2 < batches)
        def _():
            orb_copy(batch + 2, which).start()

    def build_pair(pair, carry):
        for which in range(2):
            build(pair * 2 + which, which)
        return carry

    both = tuple(range(HALVES))
    for half in both:
        loaded(half)
        if square:
            swap_copy(half).start()
        pass_on(0, half)
    over(1, group, tile_copy, wait)
    to_table = pltpu.make_async_copy(tables, table, local_sem.at[1])
    to_table.start()
    to_table.wait()
    for half in both:
        if square:
            trade(half, True)
        else:
            send_picks(0, half)
    for batch in range(batches):
        found = jnp.full((8, LANES), list_len, jnp.int32)
        for spot in range(list_len):
            found = jnp.where(lane == places[lists[spot, batch]], spot, found)
        own_inv[batch : batch + 1, :] = found[0:1]
    to_inv = pltpu.make_async_copy(own_inv, inv, local_sem.at[3])
    to_inv.start()
    to_inv.wait()
    lax.fori_loop(0, batches // 2, build_pair, 0)
    if batches % 2:
        build(batches - 1, 0)
    if square:
        for half in both:
            swap_copy(half).wait_recv()
            trade(half, False)
    for step in range(1, steps):
        middle = group // 2 if step > 1 else 0
        pass_on(step, 0)
        send_picks(step, 0)
        density_pieces(step - 1, both, 0, middle)
        pass_on(step, 1)
        send_picks(step, 1)
        density_pieces(step - 1, both, middle, group - 1)
        density_piece(step - 1, both, 0)
    if square:
        for half in both:
            swap_copy(half).wait_send()
    for half in both:
        if half == 1:
            sent_on()
        density_piece(steps - 1, (half,), 0)
        density_pieces(steps - 1, (half,), 0, group - 1)

    load_harms.wait()
    load_weights.wait()

    def live_row(batch):
        point = lax.broadcasted_iota(jnp.int32, (1, points), 1)
        return jnp.where(
            point < counts[batch], weights[pl.ds(batch, 1), :], jnp.float32(0.0)
        )

    components = harms.shape[1]
    moment = jnp.zeros((components, points), jnp.float32)
    for batch in range(batches):
        across = slice(batch * points, (batch + 1) * points)
        dens = jnp.sum(rho[:, across], axis=0, keepdims=True)
        rho[0:1, across] = dens
        moment += harms[batch].astype(jnp.float32) * (live_row(batch) * dens)
    diagonal = lax.broadcasted_iota(jnp.int32, (components, LANES), 0) == lax.broadcasted_iota(
        jnp.int32, (components, LANES), 1
    )
    summed = jnp.sum(moment, axis=1, keepdims=True)
    line = jnp.sum(jnp.where(diagonal, summed, 0.0), axis=0, keepdims=True)
    share[...] = jnp.broadcast_to(line, share.shape)
    whose, _ = any_device(0)
    shares[whose] = jnp.broadcast_to(line, share.shape)
    over(1, devices, share_copy, start)
    for half in both:
        for step in range(max(0, steps - 2), steps):
            over_blocks(step, half, wait_send)
    over(1, devices, share_copy, wait)
    line = jnp.sum(shares[...], axis=0)[0:1]
    total_moment = jnp.sum(jnp.where(diagonal, line, 0.0), axis=1, keepdims=True)
    for batch in range(batches):
        across = slice(batch * points, (batch + 1) * points)
        dens = rho[0:1, across]
        far = FAR_COEFF * jnp.sum(
            total_moment * harms[batch].astype(jnp.float32), axis=0, keepdims=True
        )
        sixth = jnp.exp(jnp.log(1.0 + dens * dens) * (1.0 / 6.0))
        potential = 0.5 * dens - sixth + far / far_scale
        factor[:, across] = jnp.broadcast_to(live_row(batch) * potential, (8, points))

    def scale_rows(step, across, where):
        ring = lax.rem(ring_me - 1 - step + 2 * steps, steps)
        owner = (ring * inner + across) * row_cap
        spots = [table[mine, 4, owner + rr] for rr in range(row_cap)]

        def chunk(index, carry):
            span = pl.ds(pl.multiple_of(index * CHUNK, CHUNK), CHUNK)
            for rr in range(row_cap):
                mate = phi[spots[rr], :, span]
                scaled = mate.astype(jnp.float32) * factor[0:1, span]
                rows[where, rr * BLK : (rr + 1) * BLK, span] = scaled.astype(rows.dtype)
            return carry

        lax.fori_loop(0, all_points // CHUNK, chunk, 0, unroll=True)

    def integral_piece(along, where, put):
        down = pl.ds(along * col_cap, col_cap)
        term = lax.dot_general(
            rows[where],
            phi[down].reshape(broad, all_points),
            (((1,), (1,)), ((), ())),
            preferred_element_type=jnp.float32,
        )
        for rr in range(row_cap):
            for cr in range(col_cap):
                value = term[rr * BLK : (rr + 1) * BLK, cr * BLK : (cr + 1) * BLK]
                put(rr * col_cap + cr, value.astype(chosen.dtype))

    def send_integrals(step):
        if step >= 2:
            for half in both:
                over_blocks(step - 2, half, wait_send, plain=True)

        def piece(place, where):
            _, along = target(place)

            def put(index, value):
                for half in both:
                    chosen[step % 2, half, place, index] = value[half * HALF : (half + 1) * HALF]

            integral_piece(along, where, put)

        def far_rows(count, carry):
            shift = inner - 1 - count

            @pl.when(count > 0)
            def _():
                scale_rows(step, lax.rem(inner_me + shift, inner), 0)

            def body(index, inner_carry):
                place = shift * narrow + narrow - 1 - index

                @pl.when(place < group - 1)
                def _():
                    piece(place, 0)

                @pl.when(place < group - 2)
                def _():
                    block_copy(step, 0, place + 1).start()

                return inner_carry

            lax.fori_loop(0, narrow, body, 0)
            return carry

        scale_rows(step, lax.rem(inner_me + inner - 1, inner), 0)
        piece(group - 1, 0)
        if inner > 1:
            scale_rows(step, inner_me, 1)
        block_copy(step, 0, group - 1).start()
        lax.fori_loop(0, inner - 1, far_rows, 0)
        home = 1 if inner > 1 else 0

        def near(index, carry):
            place = narrow - 1 - index

            @pl.when(place < group - 1)
            def _():
                piece(place, home)

            @pl.when(place < group - 2)
            def _():
                block_copy(step, 0, place + 1).start()

            return carry

        lax.fori_loop(0, narrow - 1, near, 0)

        def put_own(index, value):
            for half in both:
                arrs[step][half][mine * cap + index] = value[half * HALF : (half + 1) * HALF]

        integral_piece(narrow_me, home, put_own)
        if group > 2:
            block_copy(step, 0, 1).start()

        def later(count, carry):
            block_copy(step, 1, group - 1 - count).start()
            return carry

        lax.fori_loop(0, group - 1, later, 0)

    def out_copy(half, piece):
        first = pl.multiple_of(piece * BLK + half * HALF, HALF)
        return pltpu.make_async_copy(
            ostage.at[piece], out_ref.at[pl.ds(first, HALF)], out_sem.at[piece]
        )

    def add_up(step, half):
        last = step == steps - 1
        ring = lax.rem(ring_me - 1 - step + 2 * steps, steps)
        over(1, group, functools.partial(block_copy, step, half), wait_recv)
        for piece in range(row_blocks):
            if step > 0:
                ring_copy(step - 1, half, piece).wait_recv()
            bases = [
                table[one, 2, (ring * inner + inner_me) * row_blocks + piece] + one * cap
                for one in range(group)
            ]

            def add_block(block, carry, piece=piece, bases=bases):
                spot = piece * col_blocks + block
                if step > 0:
                    total = raws[step][half][spot].astype(jnp.float32)
                else:
                    total = jnp.zeros((HALF, BLK), jnp.float32)
                for one in range(group):
                    col = table[one, 3, narrow_me * col_blocks + block]
                    place = jnp.minimum(bases[one] + col, empty)
                    total += arrs[step][half][place].astype(jnp.float32)
                if last:
                    across = pl.ds(pl.multiple_of(block * BLK, BLK), BLK)
                    ostage[piece, :, across] = total
                else:
                    raws[step][half][spot] = total.astype(chosen.dtype)
                return carry

            lax.fori_loop(0, col_blocks, add_block, 0)
            if last:
                out_copy(half, piece).start()
            elif piece > 0:
                ring_copy(step, half, piece - 1).start()
        if not last:
            ring_copy(step, half, row_blocks - 1).start()
        else:
            if half == 1:
                over_blocks(step, half, wait_send, plain=True)
            for piece in range(row_blocks):
                out_copy(half, piece).wait()

    send_integrals(0)
    for step in range(steps):
        add_up(step, 0)
        if step + 1 < steps:
            send_integrals(step + 1)
        else:
            sent_on()
            if steps > 1:
                for half in both:
                    over_blocks(step - 1, half, wait_send, plain=True)
            over_blocks(step, 0, wait_send, plain=True)
        add_up(step, 1)


def whole_step(
    block_slot, region_blocks, lists, counts, weights, dens, orbitals, harmonics, steps, inner, narrow, caps, far_scale
):
    row_cap, col_cap = caps
    group = inner * narrow
    cap = row_cap * col_cap
    devices = steps * group
    ring_sems = max(1, steps - 1)
    row_blocks, col_blocks = dens.shape[0] // BLK, dens.shape[1] // BLK
    held = row_blocks * col_blocks
    batches, list_len, _, points = orbitals.shape
    all_points = batches * points
    components = harmonics.shape[1]
    slots = narrow * col_cap
    ints = jnp.int32
    anywhere = pl.BlockSpec(memory_space=pl.ANY)
    dma = pltpu.SemaphoreType.DMA
    swap_scratch = []
    if trades(inner, narrow):
        swap_scratch = [pltpu.VMEM((held, HALF, BLK), dens.dtype)] * HALVES
        swap_scratch += [dma((HALVES,)), dma((HALVES,))]
    return pl.pallas_call(
        functools.partial(step_kernel, steps, inner, narrow, row_cap, col_cap, far_scale),
        out_shape=jax.ShapeDtypeStruct(dens.shape, jnp.float32),
        in_specs=[anywhere] * 8,
        out_specs=anywhere,
        scratch_shapes=[pltpu.VMEM((held, HALF, BLK), dens.dtype)] * (steps * HALVES)
        + [pltpu.VMEM((group * cap + 1, HALF, BLK), dens.dtype)] * (steps * HALVES)
        + swap_scratch
        + [
            pltpu.VMEM((2, HALVES, group, cap, HALF, BLK), dens.dtype),
            pltpu.SMEM(block_slot.shape, ints),
            pltpu.SMEM(region_blocks.shape, ints),
            pltpu.SMEM(lists.shape, ints),
            pltpu.SMEM(counts.shape, ints),
            pltpu.VMEM(weights.shape, weights.dtype),
            pltpu.SMEM(region_blocks.shape, ints),
            pltpu.VMEM((8, LANES), ints),
            pltpu.VMEM((-(-batches // 8) * 8, LANES), ints),
            pltpu.SMEM((-(-batches // 8) * 8, LANES), ints),
            pltpu.VMEM((group, 8, LANES), ints),
            pltpu.SMEM((group, 8, LANES), ints),
            pltpu.VMEM((list_len + 1, BLK, points), orbitals.dtype),
            pltpu.VMEM((list_len + 1, BLK, points), orbitals.dtype),
            pltpu.VMEM((slots + 1, BLK, all_points), orbitals.dtype),
            pltpu.VMEM((2, row_cap * BLK, all_points), orbitals.dtype),
            pltpu.VMEM(harmonics.shape, harmonics.dtype),
            pltpu.VMEM((8, all_points), jnp.float32),
            pltpu.VMEM((8, all_points), jnp.float32),
            pltpu.VMEM((8, LANES), jnp.float32),
            pltpu.VMEM((devices, 8, LANES), jnp.float32),
            pltpu.VMEM((row_blocks, HALF, dens.shape[1]), jnp.float32),
            dma((steps, HALVES, group)),
            dma((steps, HALVES, group)),
            dma((ring_sems, HALVES, row_blocks)),
            dma((ring_sems, HALVES, row_blocks)),
            dma((HALVES,)),
            dma((group,)),
            dma((group,)),
            dma((2,)),
            dma((4,)),
            dma((4,)),
            dma((devices,)),
            dma((devices,)),
            dma((row_blocks,)),
        ],
        compiler_params=pltpu.CompilerParams(
            collective_id=1, has_side_effects=True, vmem_limit_bytes=VMEM_BYTES
        ),
        name="grid_step",
    )(block_slot, region_blocks, lists, counts, weights, dens, orbitals, harmonics)


def settle_kernel(given_ref, out_ref, held, sems):
    chunks, size = held.shape[0], held.shape[1]

    def copy(index, out):
        span = pl.ds(index * size, size)
        if out:
            return pltpu.make_async_copy(held.at[index], out_ref.at[span], sems.at[1, index])
        return pltpu.make_async_copy(given_ref.at[span], held.at[index], sems.at[0, index])

    for index in range(chunks):
        copy(index, False).start()
    for index in range(chunks):
        copy(index, False).wait()
        copy(index, True).start()
    for index in range(chunks):
        copy(index, True).wait()


def settle(result):
    chunks = 8
    rows, cols = result.shape
    anywhere = pl.BlockSpec(memory_space=pl.ANY)
    return pl.pallas_call(
        settle_kernel,
        out_shape=jax.ShapeDtypeStruct(result.shape, result.dtype),
        in_specs=[anywhere],
        out_specs=anywhere,
        scratch_shapes=[
            pltpu.VMEM((chunks, rows // chunks, cols), result.dtype),
            pltpu.SemaphoreType.DMA((2, chunks)),
        ],
        compiler_params=pltpu.CompilerParams(vmem_limit_bytes=VMEM_BYTES),
        name="settle",
    )(result)


def per_device(
    region, density, block_slot, region_blocks, basis_lists, point_counts, orbitals, weights, harmonics
):
    wide = lax.axis_size("wide")
    narrow = lax.axis_size("narrow")
    devices = wide * narrow
    steps = math.gcd(wide, RING)
    inner = wide // steps
    row_cap = max(1, region // wide)
    col_cap = region // narrow

    components = harmonics.shape[1]
    batches, _, points = orbitals.shape
    total_points = batches * points * devices
    result = whole_step(
        block_slot,
        region_blocks,
        basis_lists.T,
        point_counts,
        weights,
        density,
        orbitals.reshape(batches, -1, BLK, points),
        harmonics,
        steps,
        inner,
        narrow,
        (row_cap, col_cap),
        math.sqrt(total_points * components),
    )
    return settle(result)


def solution(mesh):
    devices = mesh.shape["wide"] * mesh.shape["narrow"]

    def whole(density, block_slot, region_blocks, *others):
        region = region_blocks.shape[0] // devices
        in_specs = (
            P("wide", "narrow"),
            P(),
            P(("wide", "narrow")),
            P(("wide", "narrow"), None),
            P(("wide", "narrow")),
            P(("wide", "narrow"), None, None),
            P(("wide", "narrow"), None),
            P(("wide", "narrow"), None, None),
        )
        mapped = jax.shard_map(
            functools.partial(per_device, region),
            mesh=mesh,
            in_specs=in_specs,
            out_specs=P("wide", "narrow"),
            check_vma=False,
        )
        return mapped(density, block_slot, region_blocks, *others)

    return whole
```
